32 devices in a mesh: groups: 2 (over y), dev: 8 (over z, x), sub: 2 (over core).
Axes of the slice: x: 2, y: 2, z: 4, core: 2. Of those that a mesh axis runs over, the one named last changes fastest.
Arguments:
- tokens: bfloat16 [2048, 2048], P(('groups', 'dev')), parts along dimension 0, may hold values from -6 to 6
- query_key_value: bfloat16 [2048, 3, 2048], P(('groups', 'dev'), None, 'sub'), parts along dimension 0, may hold values from -6 to 6
- out_weight: bfloat16 [2048, 2048], P('dev', 'sub'), may hold values from -0.125 to 0.125
- modulation: float32 [8, 2048], P('groups'), parts along dimension 0, may hold values from -3 to 3
- router_weight: bfloat16 [2048, 64], replicated, may hold values from -0.125 to 0.125
- expert_ids: int32 [2048, 4], P(('groups', 'dev')), parts along dimension 0, may hold values from 0 to 63, all different within a row; in each aligned block of 128 rows (0 to 127, 128 to 255, ...) at most 12 rows name the same one
- gate_up_weight: bfloat16 [128, 2, 2048, 384], P('dev', None, None, 'sub'), may hold values from -0.125 to 0.125
- down_weight: bfloat16 [128, 384, 2048], P('dev', None, 'sub'), may hold values from -0.21875 to 0.21875
Outputs:
- block_out: bfloat16 [2048, 2048], P(('groups', 'dev'), 'sub'), parts along dimension 0
The draws below stay inside these ranges and needn't reach their ends.
There are 2 independent parts, one for each index of `groups`. The reference program is written for one: setup_inputs(seed, part) draws one part's arguments, and reference() takes and returns one part's arrays. A program takes and returns all parts, laid end to end along the dimension named above; an argument that names none is the same for every part. Nothing has to cross between parts.
Inputs may be any that keep to these rules, and one draw needn't show every extreme that they name: `expert_ids`: each token names 4 different experts. Within each aligned block of 128 rows no expert is named by more than 12 rows, a bound that some block reaches.
All inputs are finite; a program needn't handle non-finite values.
Results may differ from the reference program's by a relative error of at most 0.008.
Values may be sent and summed in bfloat16 or wider, within the bound.
A program may use at most 128 MiB of HBM per device.

```python
import math
import jax
import jax.numpy as jnp
import numpy as np
from jax import lax

D = 2048
HEADS = 16
HEAD = 128
FF = 768
EXPERTS = 64
TOPK = 4
TOK_DEV = 128
CAP = 12
TOKENS = 1024
N_DEV = 8


def draw_query_key_value(key, part):
    base_key = jax.random.fold_in(jax.random.fold_in(key, 7331), 0)
    width = HEADS * HEAD
    values = jnp.clip(jax.random.normal(base_key, (TOKENS, 3, width), jnp.float32), -6.0, 6.0)
    return values.astype(jnp.bfloat16)


def steps_of(stream_key, dims, cuts, smallest, top_value):
    def one(axis_at, blocks):
        heights = jax.random.uniform(jax.random.fold_in(jax.random.fold_in(stream_key, 6), axis_at), (blocks,), jnp.float32, smallest / len(cuts), top_value / len(cuts))
        return jnp.repeat(jnp.exp(heights), dims[axis_at] // blocks).reshape((-1,) + (1,) * (len(dims) - axis_at - 1))

    loudness = one(*cuts[0])
    for cut in cuts[1:]:
        loudness = loudness * one(*cut)
    return loudness


def routed_block(own_key, own, number, rows, amount, top, most, lean):
    ranking = jax.random.permutation(own_key, amount)
    crowded, ordinary = load_shares(amount, rows * top, most, lean, True), load_shares(amount, rows * top, most, lean, False)
    places = jnp.arange(amount)

    def named(tallies, turn):
        used = int((tallies > 0).sum())
        fixed = max(1, used // 4)
        shifted = fixed + (places - fixed + turn * (used - fixed)) % max(1, amount - fixed)
        return jnp.zeros((amount,), jnp.int32).at[ranking[jnp.where(places < fixed, places, shifted)]].set(jnp.asarray(tallies, jnp.int32))

    tallies = jnp.where(number % 4 == 0, named(crowded, number // 4), named(ordinary, number - number // 4 - 1))
    mixed = jax.random.permutation(jax.random.fold_in(own, 3), amount)
    giver, receiver = mixed[0:amount // 2 * 2:2], mixed[1:amount // 2 * 2:2]
    room = jnp.minimum(tallies[giver] - 1, most - tallies[receiver]) // 2
    room = jnp.where((giver == ranking[0]) | (receiver == ranking[0]) | (tallies[receiver] == 0), 0, jnp.maximum(room, 0))
    shifted = jax.random.randint(jax.random.fold_in(own, 4), (amount // 2,), 0, 1 << 20) % (room + 1)
    tallies = tallies.at[giver].add(-shifted).at[receiver].add(shifted)
    members = jnp.searchsorted(jnp.cumsum(tallies), jnp.arange(rows * top), side="right").astype(jnp.int32)
    listing = members.reshape(top, rows).T
    listing = listing[jax.random.permutation(jax.random.fold_in(own, 1), rows)]
    turn = jax.random.randint(jax.random.fold_in(own, 2), (rows, 1), 0, top)
    return jnp.take_along_axis(listing, (jnp.arange(top)[None, :] + turn) % top, axis=1)


def load_shares(number_of, total, most, slope, full):
    portions = [(1 << 20) // math.isqrt(rank ** slope) + 1 for rank in range(1, number_of + 1)]
    largest = most if full else min(most, max(-(-total // number_of), total * portions[0] // sum(portions)))
    least = 1 if total - largest >= number_of - 1 else 0
    given, rest = [largest] + [least] * (number_of - 1), total - largest - least * (number_of - 1)
    while rest > 0:
        candidates = [i for i in range(1, number_of) if given[i] < largest] or [i for i in range(1, number_of) if given[i] < most]
        whole, remaining = sum([portions[i] for i in candidates]), rest
        for i in candidates:
            more = min(most - given[i], max(1, remaining * portions[i] // whole), rest)
            given[i] = given[i] + more
            rest = rest - more
    return np.array(given)


def gaussian(stream_key, dims, deviation, limit, cuts=(), kind=jnp.bfloat16):
    entries = jax.random.normal(stream_key, dims, jnp.float32) * deviation
    if len(cuts) > 0:
        entries = steps_of(stream_key, dims, cuts, -0.22, 0.18) * entries
    return jnp.clip(entries, min=-limit, max=limit).astype(kind)


def setup_inputs(seed: int = 0, part: int = 0) -> dict:
    key_list = jax.random.split(jax.random.key(seed), 9)
    part_splits = jax.random.split(jax.random.fold_in(key_list[8], part), 9)
    tokens = gaussian(part_splits[0], (TOKENS, D), 1.0, 6.0, ((0, 8),))
    query_key_value = draw_query_key_value(jax.random.fold_in(jax.random.fold_in(key_list[8], part), 71), part)
    out_weight = gaussian(key_list[2], (D, HEADS * HEAD), (HEADS * HEAD) ** -0.5, 0.125, ((0, 8), (1, 2)))
    modulation = gaussian(part_splits[3], (4, D), 0.5, 3.0, (), jnp.float32)
    router_weight = gaussian(key_list[4], (D, EXPERTS), D ** -0.5, 0.125)
    expert_ids_keys = jax.random.split(jax.random.fold_in(part_splits[5], 1), TOKENS // TOK_DEV)
    expert_ids_turns = jax.random.permutation(jax.random.fold_in(part_splits[5], 3), TOKENS // TOK_DEV)
    expert_ids = jax.vmap(lambda own, number: routed_block(jax.random.fold_in(part_splits[5], 2), own, number, TOK_DEV, EXPERTS, TOPK, CAP, 1))(expert_ids_keys, expert_ids_turns).reshape((TOKENS, TOPK))
    gate_up_weight = gaussian(key_list[6], (2 * EXPERTS, 2, D, FF // 2), D ** -0.5, 0.125, ((0, 8), (3, 2)))
    down_weight = gaussian(key_list[7], (2 * EXPERTS, FF // 2, D), FF ** -0.5, 0.21875, ((0, 8), (2, 2)))
    return {"tokens": tokens, "query_key_value": query_key_value, "out_weight": out_weight, "modulation": modulation, "router_weight": router_weight, "expert_ids": expert_ids, "gate_up_weight": gate_up_weight, "down_weight": down_weight}


EPS = 1e-06
NEG = -1e+30

def window_attention(query, keys, values, index, total):
    count = query.shape[0]
    rows = jnp.arange(count, dtype=jnp.int32)[:, None]
    cols = jnp.arange(3 * count, dtype=jnp.int32)[None, :] - count
    place = index * count + cols
    allowed = (jnp.abs(cols - rows) <= count) & (place >= 0) & (place < total)
    scores = jnp.einsum('qhd,khd->hqk', query.astype(jnp.float32), keys.astype(jnp.float32)) / math.sqrt(query.shape[2])
    scores = jnp.where(allowed[None], scores, NEG)
    top = lax.optimization_barrier(jnp.max(scores, -1, keepdims=True))
    weight = jnp.exp(scores - top)
    weight = (weight / lax.optimization_barrier(jnp.sum(weight, -1, keepdims=True))).astype(jnp.bfloat16)
    mixed = jnp.einsum('hqk,khd->qhd', weight.astype(jnp.float32), values.astype(jnp.float32))
    return mixed.astype(jnp.bfloat16)

def attend(query_key_value):
    blocks = TOKENS // TOK_DEV
    packed = query_key_value.reshape(blocks, TOK_DEV, 3, HEADS, HEAD)
    empty = jnp.zeros((1, TOK_DEV, 3, HEADS, HEAD), packed.dtype)
    padded = jnp.concatenate([empty, packed, empty], 0)

    def block(index):
        near = lax.dynamic_slice_in_dim(padded, index, 3, 0).reshape(3 * TOK_DEV, 3, HEADS, HEAD)
        query = lax.dynamic_index_in_dim(packed, index, 0, keepdims=False)[:, 0]
        return window_attention(query, near[:, 1], near[:, 2], index, TOKENS)
    result = lax.map(block, jnp.arange(blocks, dtype=jnp.int32))
    return result.reshape(TOKENS, HEADS * HEAD)

def normalize(state, modulation):
    scale = lax.rsqrt(lax.optimization_barrier(jnp.mean(state * state, -1, keepdims=True)) + EPS)
    return (state * scale * (1.0 + modulation[2]) + modulation[1]).astype(jnp.bfloat16)

def route(normed, router_weight, expert_ids):
    logits = jnp.dot(normed, router_weight, preferred_element_type=jnp.float32)
    experts = router_weight.shape[1]
    match = expert_ids[:, :, None] == jnp.arange(experts, dtype=jnp.int32)[None, None, :]
    picked = lax.optimization_barrier(jnp.sum(jnp.where(match, logits[:, None, :], 0.0), -1))
    lifted = jax.nn.sigmoid(picked)
    return lifted / lax.optimization_barrier(jnp.sum(lifted, -1, keepdims=True))

def experts_sum(normed, gates, expert_ids, gate_up_weight, down_weight):
    room = N_DEV * CAP

    def step(total, expert):
        match = expert_ids == expert
        chosen = jnp.any(match, 1)
        rows = jnp.nonzero(chosen, size=room, fill_value=0)[0].astype(jnp.int32)
        live = jnp.arange(room, dtype=jnp.int32) < jnp.sum(chosen.astype(jnp.int32))
        weight = lax.optimization_barrier(jnp.sum(jnp.where(match, gates, 0.0), 1))[rows]
        weight = jnp.where(live, weight, 0.0)
        pair = lax.dynamic_slice_in_dim(gate_up_weight, 2 * expert, 2, 0)
        down_pair = lax.dynamic_slice_in_dim(down_weight, 2 * expert, 2, 0)
        inputs = normed[rows]
        output = jnp.zeros((room, normed.shape[1]), jnp.float32)
        for half in range(2):
            gate = jnp.dot(inputs, pair[half, 0], preferred_element_type=jnp.float32)
            up = jnp.dot(inputs, pair[half, 1], preferred_element_type=jnp.float32)
            hidden = (jax.nn.silu(gate) * up).astype(jnp.bfloat16)
            piece = jnp.dot(hidden, down_pair[half], preferred_element_type=jnp.float32).astype(jnp.bfloat16)
            output = output + piece.astype(jnp.float32)
        return (total.at[rows].add(weight[:, None] * output), None)
    total = jnp.zeros((normed.shape[0], normed.shape[1]), jnp.float32)
    total, _ = lax.scan(step, total, jnp.arange(EXPERTS, dtype=jnp.int32))
    return total

def reference(tokens, query_key_value, out_weight, modulation, router_weight, expert_ids, gate_up_weight, down_weight):
    mixed = attend(query_key_value)
    proj = lax.dot_general(mixed, out_weight, (((1,), (1,)), ((), ())), preferred_element_type=jnp.float32)
    state = tokens.astype(jnp.float32) + (1.0 + modulation[0]) * proj
    normed = normalize(state, modulation)
    gates = route(normed, router_weight, expert_ids)
    routed = experts_sum(normed, gates, expert_ids, gate_up_weight, down_weight)
    return (state + (1.0 + modulation[3]) * routed).astype(jnp.bfloat16)
```

```python
import functools
import math

import jax
import jax.numpy as jnp
from jax import lax
from jax.experimental import pallas as pl
from jax.experimental.pallas import tpu as pltpu
from jax.sharding import PartitionSpec as P

HEAD = 128
CAP = 12


EPS = 1e-06
NEG = -1e30


def extended(cells, sides, width):
    for axis, dim in sides:
        count = lax.axis_size(axis)
        ends = count - 1
        head = lax.slice_in_dim(cells, 0, width, axis=dim)
        tail = lax.slice_in_dim(cells, cells.shape[dim] - width, cells.shape[dim], axis=dim)
        cells = jnp.concatenate(
            [
                lax.ppermute(tail, axis, [(i, (i + 1) % count) for i in range(ends)]),
                cells,
                lax.ppermute(head, axis, [((i + 1) % count, i) for i in range(ends)]),
            ],
            axis=dim,
        )
    return cells


def window_attention(query, keys, values, index, total):
    count = query.shape[0]
    rows = jnp.arange(count, dtype=jnp.int32)[:, None]
    cols = jnp.arange(3 * count, dtype=jnp.int32)[None, :] - count
    place = index * count + cols
    allowed = (jnp.abs(cols - rows) <= count) & (place >= 0) & (place < total)
    scores = jnp.einsum(
        "qhd,khd->hqk", query, keys, preferred_element_type=jnp.float32
    ) / math.sqrt(query.shape[2])
    scores = jnp.where(allowed[None], scores, NEG)
    top = jnp.max(scores, -1, keepdims=True)
    weight = jnp.exp(scores - top)
    weight = (weight / jnp.sum(weight, -1, keepdims=True)).astype(jnp.bfloat16)
    mixed = jnp.einsum("hqk,khd->qhd", weight, values, preferred_element_type=jnp.float32)
    return mixed.astype(jnp.bfloat16)


def normalize(state, modulation):
    scale = lax.rsqrt(jnp.mean(state * state, -1, keepdims=True) + EPS)
    return (state * scale * (1.0 + modulation[2]) + modulation[1]).astype(jnp.bfloat16)


def route(normed, router_weight, expert_ids):
    logits = jnp.dot(normed, router_weight, preferred_element_type=jnp.float32)
    experts = router_weight.shape[1]
    match = expert_ids[:, :, None] == jnp.arange(experts, dtype=jnp.int32)[None, None, :]
    picked = jnp.sum(jnp.where(match, logits[:, None, :], 0.0), -1)
    lifted = jax.nn.sigmoid(picked)
    return lifted / jnp.sum(lifted, -1, keepdims=True)


LANES = 128
SLOT = 16
COLS = 2
VMEM_BYTES = 66 * 1000 * 1000
MESH = pl.DeviceIdType.MESH


def expert_kernel(
    rows_of, devices,
    normed, meta, state, modulation, gate_up, down,
    out,
    tok, disp, gu, dn, hid_own, hid_other, got_meta, pick, slot_gate, got_x, got_up, got_down, acc,
    meta_s, meta_r, ag_s, ag_r, core_r, gu_sem, dn_sem, hid_s, hid_r,
    x_s, x_r, up_s, up_r, down_s, down_r,
):
    me = lax.axis_index("dev")
    part = lax.axis_index("sub")
    other = 1 - part
    z = me // COLS
    x = me % COLS
    across = z * COLS + (1 - x)
    lines = devices // COLS
    count, width = normed.shape
    half = width // 2
    halves = gate_up.shape[0]
    local = halves // 2
    hidden = gate_up.shape[2]
    slots = local * SLOT

    def weight_copies(h):
        return (
            pltpu.make_async_copy(gate_up.at[h], gu.at[h], gu_sem.at[h]),
            pltpu.make_async_copy(down.at[h], dn.at[h], dn_sem.at[h]),
        )

    barrier = pltpu.get_barrier_semaphore()
    for step in range(1, devices):
        pl.semaphore_signal(
            barrier, inc=1, device_id={"dev": (me + step) % devices}, device_id_type=MESH
        )
    pl.semaphore_signal(barrier, inc=1, device_id={"sub": other}, device_id_type=MESH)
    pl.semaphore_wait(barrier, devices)

    def remote(src, dst, send, recv, where):
        return pltpu.make_async_remote_copy(
            src_ref=src, dst_ref=dst, send_sem=send, recv_sem=recv,
            device_id=where, device_id_type=MESH,
        )

    def block(s, way, where, src=None):
        dst = tok.at[part, s]
        recv = core_r.at[s] if way == 3 else ag_r.at[s]
        return remote(dst if src is None else src, dst, ag_s.at[s, way], recv, where)

    up_to = {"dev": jnp.minimum(me + COLS, devices - 1)}
    down_to = {"dev": jnp.maximum(me - COLS, 0)}
    x_to = {"dev": across}
    core_to = {"sub": other}
    not_top = z < lines - 1
    not_bottom = z > 0
    mine = normed.at[:, pl.ds(pl.multiple_of(part * half, LANES), half)]

    def meta_copy(step):
        target = (me + step) % devices
        return remote(
            meta.at[pl.ds(pl.multiple_of(target * local, local), local)], got_meta.at[me],
            meta_s.at[step - 1], meta_r.at[me], {"dev": target},
        )

    for step in range(1, devices):
        meta_copy(step).start()

    @pl.when(not_top)
    def _():
        block(me, 0, up_to, mine).start()

    @pl.when(not_bottom)
    def _():
        block(me, 1, down_to, mine).start()

    block(me, 2, x_to, mine).start()

    def start_weights(h, carry):
        for copy in weight_copies(h):
            copy.start()
        return carry

    lax.fori_loop(0, halves, start_weights, 0)

    before = (
        lax.broadcasted_iota(jnp.int32, (count, count), 0)
        < lax.broadcasted_iota(jnp.int32, (count, count), 1)
    ).astype(jnp.float32).astype(jnp.bfloat16)
    place = lax.broadcasted_iota(jnp.int32, (local, SLOT, count), 1).astype(jnp.float32)

    def routing(s, gate):
        chosen = jnp.where(gate > 0.0, 1.0, 0.0)
        rank = jnp.dot(chosen.astype(jnp.bfloat16), before, preferred_element_type=jnp.float32)
        rank = jnp.where(gate > 0.0, rank, -1.0)
        hit = jnp.broadcast_to(rank[:, None, :], place.shape) == place
        pick[s] = jnp.where(hit, 1.0, 0.0).reshape(slots, count).astype(jnp.bfloat16)
        value = jnp.where(hit, jnp.broadcast_to(gate[:, None, :], place.shape), 0.0)
        value = jnp.sum(value, -1, keepdims=True)
        slot_gate[:, pl.ds(pl.multiple_of(s * SLOT, SLOT), SLOT), :] = jnp.broadcast_to(
            value, (local, SLOT, LANES)
        )

    def dispatch(s, h, rows):
        moved = jnp.dot(pick[s], rows, preferred_element_type=jnp.float32)
        disp[h, :, pl.ds(pl.multiple_of(s * SLOT, SLOT), SLOT), :] = moved.astype(
            jnp.bfloat16
        ).reshape(local, SLOT, half)

    routing(me, meta[pl.ds(pl.multiple_of(me * local, local), local)])
    dispatch(me, 0, normed[:, :half])
    dispatch(me, 1, normed[:, half:])
    for step in range(1, devices):
        s = (me + step) % devices
        remote(
            meta.at[pl.ds(0, local)], got_meta.at[s], meta_s.at[0], meta_r.at[s], {"dev": s}
        ).wait_recv()
        routing(s, got_meta[s])

    def arrive(s):
        block(s, 2, x_to).wait_recv()

    def from_line(zz, way, where, more):
        s = zz * COLS + x
        arrive(s)

        @pl.when(more)
        def _():
            block(s, way, where).start()

        block(s, 2, x_to).start()
        block(s, 3, core_to).start()
        dispatch(s, part, tok[part, s])

    def from_across(zz):
        s = zz * COLS + (1 - x)
        arrive(s)
        block(s, 3, core_to).start()
        dispatch(s, part, tok[part, s])

    def from_core(s):
        remote(tok.at[other, s], tok.at[other, s], ag_s.at[s, 3], core_r.at[s], core_to).wait_recv()
        dispatch(s, other, tok[other, s])

    def both(d, act):
        @pl.when(z - d >= 0)
        def _():
            act(z - d, True)

        @pl.when(z + d < lines)
        def _():
            act(z + d, False)

    for d in range(1, lines):
        both(d, lambda zz, low: from_line(
            zz, 0 if low else 1, up_to if low else down_to, not_top if low else not_bottom
        ))
        if d == 1:
            from_across(z)
        else:
            both(d - 1, lambda zz, low: from_core(zz * COLS + x))
    both(lines - 1, lambda zz, low: from_core(zz * COLS + x))
    from_core(across)
    for d in range(1, lines):
        both(d, lambda zz, low: from_across(zz))
        if d > 1:
            both(d - 1, lambda zz, low: from_core(zz * COLS + (1 - x)))
    both(lines - 1, lambda zz, low: from_core(zz * COLS + (1 - x)))

    @pl.when(not_top)
    def _():
        block(me, 0, up_to, mine).wait_send()

    @pl.when(not_bottom)
    def _():
        block(me, 1, down_to, mine).wait_send()

    block(me, 2, x_to, mine).wait_send()
    for d in range(1, lines):

        def sent(zz, low):
            s = zz * COLS + x

            @pl.when(not_top if low else not_bottom)
            def _():
                block(s, 0 if low else 1, up_to).wait_send()

            block(s, 2, x_to).wait_send()
            block(s, 3, core_to).wait_send()
            block(zz * COLS + (1 - x), 3, core_to).wait_send()

        both(d, sent)
    block(across, 3, core_to).wait_send()

    def hid_copy(h):
        return remote(hid_own.at[h], hid_other.at[h], hid_s.at[h], hid_r.at[h], core_to)

    def across_rows(left, right):
        return lax.dot_general(
            left, right, (((1,), (1,)), ((), ())), preferred_element_type=jnp.float32
        )

    def raise_expert(e):
        low, high = disp[0, e], disp[1, e]
        for b in range(2):
            h = 2 * e + b
            weight_copies(h)[0].wait()

            def product(g):
                return across_rows(low, gu[h, g, :, :half]) + across_rows(high, gu[h, g, :, half:])

            gate = product(0)
            hid_own[h] = (gate * jax.nn.sigmoid(gate) * product(1)).astype(jnp.bfloat16)
            hid_copy(h).start()

    def lower_expert(e):
        total = None
        for b in range(2):
            h = 2 * e + b
            weight_copies(h)[1].wait()
            hid_copy(h).wait_recv()
            first = dn[h, pl.ds(pl.multiple_of(part * hidden, SLOT), hidden), :]
            second = dn[h, pl.ds(pl.multiple_of(other * hidden, SLOT), hidden), :]
            piece = jnp.dot(hid_own[h], first, preferred_element_type=jnp.float32) + jnp.dot(
                hid_other[h], second, preferred_element_type=jnp.float32
            )
            piece = piece.astype(jnp.bfloat16).astype(jnp.float32)
            total = piece if total is None else total + piece
        gain = slot_gate[e][:, :1]
        disp[0, e] = (total * gain).astype(jnp.bfloat16)

    raise_expert(0)

    def step_expert(e, carry):
        raise_expert(e)
        lower_expert(e - 1)
        return carry

    lax.fori_loop(1, local, step_expert, 0)
    lower_expert(local - 1)

    def combine(s):
        rows = disp[0, :, pl.ds(pl.multiple_of(s * SLOT, SLOT), SLOT), :].reshape(slots, half)
        return lax.dot_general(
            pick[s], rows, (((0,), (0,)), ((), ())), preferred_element_type=jnp.float32
        )

    def x_copy(zz):
        return remote(
            tok.at[0, zz * COLS + (1 - x)], got_x.at[zz], x_s.at[zz], x_r.at[zz], x_to
        )

    def line_copy(zz, low):
        if low:
            return remote(tok.at[1, zz], got_down.at[zz], down_s.at[zz], down_r.at[zz], down_to)
        return remote(tok.at[1, zz], got_up.at[zz], up_s.at[zz], up_r.at[zz], up_to)

    def give_across(zz, low):
        s = zz * COLS + (1 - x)
        tok[0, s] = combine(s).astype(jnp.bfloat16)
        x_copy(zz).start()

    def add_line(zz, low):
        line_copy(zz, low).wait_recv()
        acc[...] += (got_down if low else got_up)[zz].astype(jnp.float32)

    def gather_here(zz):
        acc[...] = combine(zz * COLS + x)
        x_copy(zz).wait_recv()
        acc[...] += got_x[zz].astype(jnp.float32)

    def pass_on(zz, low):
        gather_here(zz)

        @pl.when(not_top if low else not_bottom)
        def _():
            add_line(zz, low)

        tok[1, zz] = acc[...].astype(jnp.bfloat16)
        line_copy(zz, low).start()

    for d in range(lines - 1, 0, -1):
        both(d, give_across)
    give_across(z, False)
    for d in range(lines - 1, 0, -1):
        both(d, pass_on)
    gather_here(z)

    @pl.when(not_bottom)
    def _():
        add_line(z, False)

    @pl.when(not_top)
    def _():
        add_line(z, True)

    own = pl.ds(pl.multiple_of(part * half, LANES), half)
    out[...] = (state[:, own] + (1.0 + modulation[3:4, own]) * acc[...]).astype(out.dtype)

    for d in range(1, lines):

        def drained(zz, low):
            line_copy(zz, low).wait_send()
            x_copy(zz).wait_send()

        both(d, drained)
    x_copy(z).wait_send()
    for step in range(1, devices):
        meta_copy(step).wait_send()

    def hid_drain(h, carry):
        hid_copy(h).wait_send()
        return carry

    lax.fori_loop(0, halves, hid_drain, 0)


def expert_call(normed, gates, expert_ids, state, modulation, gate_up_weight, down_weight, experts):
    devices = lax.axis_size("dev")
    count, width = normed.shape
    half = down_weight.shape[2]
    halves = gate_up_weight.shape[0]
    local = halves // 2
    gate_up_weight = gate_up_weight.swapaxes(2, 3)
    hidden = gate_up_weight.shape[2]
    lines = devices // COLS
    rows = devices * SLOT
    match = expert_ids[:, None, :] == jnp.arange(experts, dtype=jnp.int32)[None, :, None]
    meta = jnp.sum(jnp.where(match, gates[:, None, :], 0.0), -1).T
    vmem = pl.BlockSpec(memory_space=pltpu.VMEM)
    hbm = pl.BlockSpec(memory_space=pl.ANY)
    dma = pltpu.SemaphoreType.DMA
    return pl.pallas_call(
        functools.partial(expert_kernel, rows, devices),
        out_shape=jax.ShapeDtypeStruct((count, half), jnp.bfloat16),
        in_specs=[vmem, vmem, vmem, vmem, hbm, hbm],
        out_specs=vmem,
        scratch_shapes=[
            pltpu.VMEM((2, devices, count, half), jnp.bfloat16),
            pltpu.VMEM((2, local, rows, half), jnp.bfloat16),
            pltpu.VMEM(gate_up_weight.shape, jnp.bfloat16),
            pltpu.VMEM(down_weight.shape, jnp.bfloat16),
            pltpu.VMEM((halves, rows, hidden), jnp.bfloat16),
            pltpu.VMEM((halves, rows, hidden), jnp.bfloat16),
            pltpu.VMEM((devices, local, count), jnp.float32),
            pltpu.VMEM((devices, local * SLOT, count), jnp.bfloat16),
            pltpu.VMEM((local, rows, LANES), jnp.float32),
            pltpu.VMEM((lines, count, half), jnp.bfloat16),
            pltpu.VMEM((lines, count, half), jnp.bfloat16),
            pltpu.VMEM((lines, count, half), jnp.bfloat16),
            pltpu.VMEM((count, half), jnp.float32),
            dma((devices,)), dma((devices,)), dma((devices, 4)), dma((devices,)), dma((devices,)),
            dma((halves,)), dma((halves,)), dma((halves,)), dma((halves,)),
            dma((lines,)), dma((lines,)), dma((lines,)), dma((lines,)), dma((lines,)), dma((lines,)),
        ],
        compiler_params=pltpu.CompilerParams(
            collective_id=1, has_side_effects=True, vmem_limit_bytes=VMEM_BYTES
        ),
    )(normed, meta, state, modulation, gate_up_weight, down_weight)


def body(
    tokens,
    query_key_value,
    out_weight,
    modulation,
    router_weight,
    expert_ids,
    gate_up_weight,
    down_weight,
):
    count = tokens.shape[0]
    width = tokens.shape[1]
    parts = lax.axis_size("sub")
    part = lax.axis_index("sub")
    position = lax.axis_index("dev")
    devices = lax.axis_size("dev")
    total = count * devices
    local_width = query_key_value.shape[2]
    heads_here = local_width // HEAD
    query = query_key_value[:, 0].reshape(count, heads_here, HEAD)
    pair = query_key_value[:, 1:]
    near = extended(pair, (("dev", 0),), count)
    keys = near[:, 0].reshape(3 * count, heads_here, HEAD)
    values = near[:, 1].reshape(3 * count, heads_here, HEAD)
    mixed = window_attention(query, keys, values, position, total).reshape(count, local_width)
    partial_proj = lax.dot_general(
        mixed,
        lax.all_gather(out_weight, "dev", axis=0, tiled=True),
        (((1,), (1,)), ((), ())),
        preferred_element_type=jnp.float32,
    )
    proj = lax.psum(partial_proj, "sub")
    state = tokens.astype(jnp.float32) + (1.0 + modulation[0]) * proj
    normed = normalize(state, modulation)
    gates = route(normed, router_weight, expert_ids)
    experts = router_weight.shape[1]
    weight_bytes = 2 * (gate_up_weight.size + down_weight.size)
    token_bytes = 10 * devices * count * width
    if devices % COLS == 0 and parts == 2 and weight_bytes + token_bytes < VMEM_BYTES:
        return expert_call(
            normed, gates, expert_ids, state, modulation, gate_up_weight, down_weight, experts
        )
    topk = expert_ids.shape[1]
    flat = expert_ids.reshape(-1)
    picks = flat.shape[0]
    onehot = (flat[:, None] == jnp.arange(experts, dtype=jnp.int32)[None, :]).astype(jnp.int32)
    rank = jnp.sum((jnp.cumsum(onehot, 0) - 1) * onehot, 1)
    target = flat * CAP + rank
    hit = target[None, :] == jnp.arange(experts * CAP, dtype=jnp.int32)[:, None]
    filled = jnp.any(hit, 1)
    anchor = jnp.sum(jnp.where(hit, jnp.arange(picks, dtype=jnp.int32)[None, :], 0), 1) // topk
    slice_width = width // parts
    sent = lax.dynamic_slice_in_dim(normed, part * slice_width, slice_width, 1)
    sent_width = sent.shape[1]
    rows_out = jnp.where(filled[:, None], sent[anchor], jnp.zeros((), jnp.bfloat16))
    halves_here = gate_up_weight.shape[0]
    doubled = jnp.broadcast_to(
        rows_out.reshape(experts, 1, CAP, sent_width), (experts, 2, CAP, sent_width)
    )
    outgoing = doubled.reshape(devices, halves_here, CAP, sent_width)
    up_form = "sxcd,xgdf->sxcgf"
    down_form = "sxcf,xfd->sxcd"
    incoming = lax.all_to_all(outgoing, "dev", split_axis=0, concat_axis=0, tiled=True)
    both = jnp.einsum(
        up_form,
        lax.all_gather(incoming, "sub", axis=3, tiled=True),
        gate_up_weight,
        preferred_element_type=jnp.float32,
    )
    hidden = (jax.nn.silu(both[..., 0, :]) * both[..., 1, :]).astype(jnp.bfloat16)
    gathered = lax.all_gather(hidden, "sub", axis=hidden.ndim - 1, tiled=True)
    result = jnp.einsum(down_form, gathered, down_weight, preferred_element_type=jnp.float32)
    returned = lax.all_to_all(
        result.astype(jnp.bfloat16), "dev", split_axis=0, concat_axis=0, tiled=True
    )
    own_width = returned.shape[-1]
    arranged = returned.reshape(experts, 2, CAP, own_width)
    answers = arranged[flat, :, rank, :].reshape(count, topk, 2, own_width).astype(jnp.float32)
    combined = answers[:, :, 0] + answers[:, :, 1]
    routed = jnp.einsum("tk,tkd->td", gates, combined)
    own = lax.dynamic_slice_in_dim(state, part * slice_width, slice_width, 1)
    lift = lax.dynamic_slice_in_dim(modulation[3], part * slice_width, slice_width, 0)
    return (own + (1.0 + lift) * routed).astype(jnp.bfloat16)


def solution(mesh):
    return jax.shard_map(
        body,
        mesh=mesh,
        in_specs=(
            P(("groups", "dev"), None),
            P(("groups", "dev"), None, "sub"),
            P("dev", "sub"),
            P("groups", None),
            P(),
            P(("groups", "dev"), None),
            P("dev", None, None, "sub"),
            P("dev", None, "sub"),
        ),
        out_specs=P(("groups", "dev"), "sub"),
        check_vma=False,
    )
```

```python
import functools
import math

import jax
import jax.numpy as jnp
from jax import lax
from jax.experimental import pallas as pl
from jax.experimental.pallas import tpu as pltpu
from jax.sharding import PartitionSpec as P

HEAD = 128
CAP = 12


EPS = 1e-06
NEG = -1e30


def extended(cells, sides, width):
    for axis, dim in sides:
        count = lax.axis_size(axis)
        ends = count - 1
        head = lax.slice_in_dim(cells, 0, width, axis=dim)
        tail = lax.slice_in_dim(cells, cells.shape[dim] - width, cells.shape[dim], axis=dim)
        cells = jnp.concatenate(
            [
                lax.ppermute(tail, axis, [(i, (i + 1) % count) for i in range(ends)]),
                cells,
                lax.ppermute(head, axis, [((i + 1) % count, i) for i in range(ends)]),
            ],
            axis=dim,
        )
    return cells


def window_attention(query, keys, values, index, total):
    count = query.shape[0]
    rows = jnp.arange(count, dtype=jnp.int32)[:, None]
    cols = jnp.arange(3 * count, dtype=jnp.int32)[None, :] - count
    place = index * count + cols
    allowed = (jnp.abs(cols - rows) <= count) & (place >= 0) & (place < total)
    scores = jnp.einsum(
        "qhd,khd->hqk", query, keys, preferred_element_type=jnp.float32
    ) / math.sqrt(query.shape[2])
    scores = jnp.where(allowed[None], scores, NEG)
    top = jnp.max(scores, -1, keepdims=True)
    weight = jnp.exp(scores - top)
    weight = (weight / jnp.sum(weight, -1, keepdims=True)).astype(jnp.bfloat16)
    mixed = jnp.einsum("hqk,khd->qhd", weight, values, preferred_element_type=jnp.float32)
    return mixed.astype(jnp.bfloat16)


def normalize(state, modulation):
    scale = lax.rsqrt(jnp.mean(state * state, -1, keepdims=True) + EPS)
    return (state * scale * (1.0 + modulation[2]) + modulation[1]).astype(jnp.bfloat16)


def route(normed, router_weight, expert_ids):
    logits = jnp.dot(normed, router_weight, preferred_element_type=jnp.float32)
    experts = router_weight.shape[1]
    match = expert_ids[:, :, None] == jnp.arange(experts, dtype=jnp.int32)[None, None, :]
    picked = jnp.sum(jnp.where(match, logits[:, None, :], 0.0), -1)
    lifted = jax.nn.sigmoid(picked)
    return lifted / jnp.sum(lifted, -1, keepdims=True)


LANES = 128
SLOT = 16
COLS = 2
VMEM_BYTES = 66 * 1000 * 1000
MESH = pl.DeviceIdType.MESH


def expert_kernel(
    devices,
    normed, meta, state, modulation, gate_up, down,
    out,
    tok, disp, gu, dn, hid_own, hid_other, got_meta, pick, slot_gate, got_x, got_up, got_down, acc,
    meta_s, meta_r, ag_s, ag_r, core_r, gu_sem, dn_sem, hid_s, hid_r,
    x_s, x_r, up_s, up_r, down_s, down_r,
):
    me = lax.axis_index("dev")
    part = lax.axis_index("sub")
    other = 1 - part
    z = me // COLS
    x = me % COLS
    across = z * COLS + (1 - x)
    lines = devices // COLS
    count, width = normed.shape
    half = width // 2
    halves = gate_up.shape[0]
    local = halves // 2
    hidden = gate_up.shape[2]
    slots = local * SLOT

    def weight_copies(h):
        return (
            pltpu.make_async_copy(gate_up.at[h], gu.at[h], gu_sem.at[h]),
            pltpu.make_async_copy(down.at[h], dn.at[h], dn_sem.at[h]),
        )

    barrier = pltpu.get_barrier_semaphore()
    for step in range(1, devices):
        pl.semaphore_signal(
            barrier, inc=1, device_id={"dev": (me + step) % devices}, device_id_type=MESH
        )
    pl.semaphore_signal(barrier, inc=1, device_id={"sub": other}, device_id_type=MESH)
    pl.semaphore_wait(barrier, devices)

    def remote(src, dst, send, recv, where):
        return pltpu.make_async_remote_copy(
            src_ref=src, dst_ref=dst, send_sem=send, recv_sem=recv,
            device_id=where, device_id_type=MESH,
        )

    def block(s, way, where, src=None):
        dst = tok.at[part, s]
        recv = core_r.at[s] if way == 3 else ag_r.at[s]
        return remote(dst if src is None else src, dst, ag_s.at[s, way], recv, where)

    up_to = {"dev": jnp.minimum(me + COLS, devices - 1)}
    down_to = {"dev": jnp.maximum(me - COLS, 0)}
    x_to = {"dev": across}
    core_to = {"sub": other}
    not_top = z < lines - 1
    not_bottom = z > 0
    mine = normed.at[:, pl.ds(pl.multiple_of(part * half, LANES), half)]

    def meta_copy(step):
        target = (me + step) % devices
        return remote(
            meta.at[pl.ds(pl.multiple_of(target * local, local), local)], got_meta.at[me],
            meta_s.at[step - 1], meta_r.at[me], {"dev": target},
        )

    for step in range(1, devices):
        meta_copy(step).start()

    @pl.when(not_top)
    def _():
        block(me, 0, up_to, mine).start()

    @pl.when(not_bottom)
    def _():
        block(me, 1, down_to, mine).start()

    block(me, 2, x_to, mine).start()

    def start_weights(h, carry):
        for copy in weight_copies(h):
            copy.start()
        return carry

    lax.fori_loop(0, halves, start_weights, 0)

    before = (
        lax.broadcasted_iota(jnp.int32, (count, count), 0)
        < lax.broadcasted_iota(jnp.int32, (count, count), 1)
    ).astype(jnp.float32).astype(jnp.bfloat16)
    place = lax.broadcasted_iota(jnp.int32, (local, SLOT, count), 1).astype(jnp.float32)

    def routing(s, gate):
        chosen = jnp.where(gate > 0.0, 1.0, 0.0)
        rank = jnp.dot(chosen.astype(jnp.bfloat16), before, preferred_element_type=jnp.float32)
        rank = jnp.where(gate > 0.0, rank, -1.0)
        hit = jnp.broadcast_to(rank[:, None, :], place.shape) == place
        pick[s] = jnp.where(hit, 1.0, 0.0).reshape(slots, count).astype(jnp.bfloat16)
        value = jnp.where(hit, jnp.broadcast_to(gate[:, None, :], place.shape), 0.0)
        value = jnp.sum(value, -1, keepdims=True)
        slot_gate[:, pl.ds(pl.multiple_of(s * SLOT, SLOT), SLOT), :] = jnp.broadcast_to(
            value, (local, SLOT, LANES)
        )

    def dispatch(s, h, rows):
        moved = jnp.dot(pick[s], rows, preferred_element_type=jnp.float32)
        disp[h, :, pl.ds(pl.multiple_of(s * SLOT, SLOT), SLOT), :] = moved.astype(
            jnp.bfloat16
        ).reshape(local, SLOT, half)

    routing(me, meta[pl.ds(pl.multiple_of(me * local, local), local)])
    dispatch(me, 0, normed[:, :half])
    dispatch(me, 1, normed[:, half:])
    for step in range(1, devices):
        s = (me + step) % devices
        remote(
            meta.at[pl.ds(0, local)], got_meta.at[s], meta_s.at[0], meta_r.at[s], {"dev": s}
        ).wait_recv()
        routing(s, got_meta[s])

    def arrive(s):
        block(s, 2, x_to).wait_recv()

    def from_line(zz, way, where, more):
        s = zz * COLS + x
        arrive(s)

        @pl.when(more)
        def _():
            block(s, way, where).start()

        block(s, 2, x_to).start()
        block(s, 3, core_to).start()
        dispatch(s, part, tok[part, s])

    def from_across(zz):
        s = zz * COLS + (1 - x)
        arrive(s)
        block(s, 3, core_to).start()
        dispatch(s, part, tok[part, s])

    def from_core(s):
        remote(tok.at[other, s], tok.at[other, s], ag_s.at[s, 3], core_r.at[s], core_to).wait_recv()
        dispatch(s, other, tok[other, s])

    def both(d, act):
        @pl.when(z - d >= 0)
        def _():
            act(z - d, True)

        @pl.when(z + d < lines)
        def _():
            act(z + d, False)

    for d in range(1, lines):
        both(d, lambda zz, low: from_line(
            zz, 0 if low else 1, up_to if low else down_to, not_top if low else not_bottom
        ))
        if d == 1:
            from_across(z)
        else:
            both(d - 1, lambda zz, low: from_core(zz * COLS + x))
    both(lines - 1, lambda zz, low: from_core(zz * COLS + x))
    from_core(across)
    for d in range(1, lines):
        both(d, lambda zz, low: from_across(zz))
        if d > 1:
            both(d - 1, lambda zz, low: from_core(zz * COLS + (1 - x)))
    both(lines - 1, lambda zz, low: from_core(zz * COLS + (1 - x)))

    @pl.when(not_top)
    def _():
        block(me, 0, up_to, mine).wait_send()

    @pl.when(not_bottom)
    def _():
        block(me, 1, down_to, mine).wait_send()

    block(me, 2, x_to, mine).wait_send()
    for d in range(1, lines):

        def sent(zz, low):
            s = zz * COLS + x

            @pl.when(not_top if low else not_bottom)
            def _():
                block(s, 0 if low else 1, up_to).wait_send()

            block(s, 2, x_to).wait_send()
            block(s, 3, core_to).wait_send()
            block(zz * COLS + (1 - x), 3, core_to).wait_send()

        both(d, sent)
    block(across, 3, core_to).wait_send()

    def hid_copy(h):
        return remote(hid_own.at[h], hid_other.at[h], hid_s.at[h], hid_r.at[h], core_to)

    def across_rows(left, right):
        return lax.dot_general(
            left, right, (((1,), (1,)), ((), ())), preferred_element_type=jnp.float32
        )

    def raise_expert(e):
        low, high = disp[0, e], disp[1, e]
        for b in range(2):
            h = 2 * e + b
            weight_copies(h)[0].wait()

            def product(g):
                return across_rows(low, gu[h, g, :, :half]) + across_rows(high, gu[h, g, :, half:])

            gate = product(0)
            hid_own[h] = (gate * jax.nn.sigmoid(gate) * product(1)).astype(jnp.bfloat16)
            hid_copy(h).start()

    def lower_expert(e):
        total = None
        for b in range(2):
            h = 2 * e + b
            weight_copies(h)[1].wait()
            hid_copy(h).wait_recv()
            first = dn[h, pl.ds(pl.multiple_of(part * hidden, SLOT), hidden), :]
            second = dn[h, pl.ds(pl.multiple_of(other * hidden, SLOT), hidden), :]
            piece = jnp.dot(hid_own[h], first, preferred_element_type=jnp.float32) + jnp.dot(
                hid_other[h], second, preferred_element_type=jnp.float32
            )
            piece = piece.astype(jnp.bfloat16).astype(jnp.float32)
            total = piece if total is None else total + piece
        gain = slot_gate[e][:, :1]
        disp[0, e] = (total * gain).astype(jnp.bfloat16)

    raise_expert(0)

    def step_expert(e, carry):
        raise_expert(e)
        lower_expert(e - 1)
        return carry

    lax.fori_loop(1, local, step_expert, 0)
    lower_expert(local - 1)

    def combine(s):
        rows = disp[0, :, pl.ds(pl.multiple_of(s * SLOT, SLOT), SLOT), :].reshape(slots, half)
        return lax.dot_general(
            pick[s], rows, (((0,), (0,)), ((), ())), preferred_element_type=jnp.float32
        )

    def x_copy(zz):
        return remote(
            tok.at[0, zz * COLS + (1 - x)], got_x.at[zz], x_s.at[zz], x_r.at[zz], x_to
        )

    def line_copy(zz, low):
        if low:
            return remote(tok.at[1, zz], got_down.at[zz], down_s.at[zz], down_r.at[zz], down_to)
        return remote(tok.at[1, zz], got_up.at[zz], up_s.at[zz], up_r.at[zz], up_to)

    def give_across(zz, low):
        s = zz * COLS + (1 - x)
        tok[0, s] = combine(s).astype(jnp.bfloat16)
        x_copy(zz).start()

    def add_line(zz, low):
        line_copy(zz, low).wait_recv()
        acc[...] += (got_down if low else got_up)[zz].astype(jnp.float32)

    def gather_here(zz):
        acc[...] = combine(zz * COLS + x)
        x_copy(zz).wait_recv()
        acc[...] += got_x[zz].astype(jnp.float32)

    def pass_on(zz, low):
        gather_here(zz)

        @pl.when(not_top if low else not_bottom)
        def _():
            add_line(zz, low)

        tok[1, zz] = acc[...].astype(jnp.bfloat16)
        line_copy(zz, low).start()

    for d in range(lines - 1, 0, -1):
        both(d, give_across)
    give_across(z, False)
    for d in range(lines - 1, 0, -1):
        both(d, pass_on)
    gather_here(z)

    @pl.when(not_bottom)
    def _():
        add_line(z, False)

    @pl.when(not_top)
    def _():
        add_line(z, True)

    own = pl.ds(pl.multiple_of(part * half, LANES), half)
    out[...] = (state[:, own] + (1.0 + modulation[3:4, own]) * acc[...]).astype(out.dtype)

    for d in range(1, lines):

        def drained(zz, low):
            line_copy(zz, low).wait_send()
            x_copy(zz).wait_send()

        both(d, drained)
    x_copy(z).wait_send()
    for step in range(1, devices):
        meta_copy(step).wait_send()

    def hid_drain(h, carry):
        hid_copy(h).wait_send()
        return carry

    lax.fori_loop(0, halves, hid_drain, 0)


def front_kernel(
    devices,
    tokens, packed, weight, modulation, router, ids,
    normed, state, meta,
    near, wide, mixed, mine_out, their_out,
    near_s, near_r, far_s, far_r, ag_s, ag_r, y_r, sum_s, sum_r,
):
    me = lax.axis_index("dev")
    part = lax.axis_index("sub")
    group = lax.axis_index("groups")
    z = me // COLS
    x = me % COLS
    across = z * COLS + (1 - x)
    lines = devices // COLS
    count, width = tokens.shape
    shard = weight.shape[0] // 2
    not_top = z < lines - 1
    not_bottom = z > 0
    up_to = {"dev": jnp.minimum(me + COLS, devices - 1)}
    down_to = {"dev": jnp.maximum(me - COLS, 0)}
    x_to = {"dev": across}
    y_to = {"groups": 1 - group}
    core_to = {"sub": 1 - part}

    barrier = pltpu.get_barrier_semaphore()
    for step in range(1, devices):
        pl.semaphore_signal(
            barrier, inc=1, device_id={"dev": (me + step) % devices}, device_id_type=MESH
        )
    pl.semaphore_signal(barrier, inc=1, device_id=core_to, device_id_type=MESH)
    pl.semaphore_signal(barrier, inc=1, device_id=y_to, device_id_type=MESH)
    pl.semaphore_wait(barrier, devices + 1)

    def remote(src, dst, send, recv, where):
        return pltpu.make_async_remote_copy(
            src_ref=src, dst_ref=dst, send_sem=send, recv_sem=recv,
            device_id=where, device_id_type=MESH,
        )

    def near_copy(i):
        return remote(packed.at[1 + i], near.at[x, i], near_s.at[i], near_r.at[i], x_to)

    def far_copy(i, where):
        return remote(near.at[1 - x, i], near.at[x, i], far_s.at[i], far_r.at[i], where)

    def piece(s, way, where, src=None):
        dst = wide.at[s, group]
        recv = y_r.at[s] if way == 3 else ag_r.at[s]
        return remote(dst if src is None else src, dst, ag_s.at[s, way], recv, where)

    far_up = (x == 0) & not_top
    far_down = (x == 1) & not_bottom
    have_far = ((x == 0) & not_bottom) | ((x == 1) & not_top)
    mine = weight.at[pl.ds(pl.multiple_of(group * shard, SLOT), shard)]

    for i in range(2):
        near_copy(i).start()

    @pl.when(not_top)
    def _():
        piece(me, 0, up_to, mine).start()

    @pl.when(not_bottom)
    def _():
        piece(me, 1, down_to, mine).start()

    piece(me, 2, x_to, mine).start()

    @pl.when(jnp.logical_not(have_far))
    def _():
        near[x] = jnp.zeros_like(near[x])

    for i in range(2):
        near_copy(i).wait_recv()

        @pl.when(far_up)
        def _():
            far_copy(i, up_to).start()

        @pl.when(far_down)
        def _():
            far_copy(i, down_to).start()

    def both(d, act):
        @pl.when(z - d >= 0)
        def _():
            act(z - d, True)

        @pl.when(z + d < lines)
        def _():
            act(z + d, False)

    def project(s, rows, block):
        mine_out[s, rows] = lax.dot_general(
            mixed[...], block, (((1,), (1,)), ((), ())), preferred_element_type=jnp.float32
        )
        sum_copy(s, rows).start()

    def sum_copy(s, rows):
        return remote(
            mine_out.at[s, rows], their_out.at[s, rows], sum_s.at[s, rows], sum_r.at[s, rows], core_to
        )

    def take_line(zz, low):
        s = zz * COLS + x
        piece(s, 2, x_to).wait_recv()

        @pl.when(not_top if low else not_bottom)
        def _():
            piece(s, 0 if low else 1, up_to if low else down_to).start()

        piece(s, 2, x_to).start()
        piece(s, 3, y_to).start()

    def take_across(zz, low):
        s = zz * COLS + (1 - x)
        piece(s, 2, x_to).wait_recv()
        piece(s, 3, y_to).start()

    def take_y(s):
        dst = wide.at[s, 1 - group]
        remote(dst, dst, ag_s.at[s, 3], y_r.at[s], y_to).wait_recv()
        project(s, 1 - group, wide[s, 1 - group])

    def use(s):
        project(s, group, wide[s, group])

    both(1, take_line)
    take_across(z, False)

    @pl.when(have_far)
    def _():
        for i in range(2):
            far_copy(i, x_to).wait_recv()

    row = lax.broadcasted_iota(jnp.int32, (count, count), 0)
    col = lax.broadcasted_iota(jnp.int32, (count, count), 1)
    see_before = (col >= row) & (me > 0)
    see_after = (col <= row) & (me < devices - 1)
    for h in range(mixed.shape[1] // HEAD):
        lanes = slice(h * HEAD, (h + 1) * HEAD)
        query = packed[0, :, lanes]

        def score(keys):
            return lax.dot_general(
                query, keys, (((1,), (1,)), ((), ())), preferred_element_type=jnp.float32
            ) / math.sqrt(HEAD)

        scores = jnp.concatenate(
            [
                jnp.where(see_before, score(near[0, 0, :, lanes]), NEG),
                score(packed[1, :, lanes]),
                jnp.where(see_after, score(near[1, 0, :, lanes]), NEG),
            ],
            axis=1,
        )
        top = jnp.max(scores, -1, keepdims=True)
        share = jnp.exp(scores - top)
        share = (share / jnp.sum(share, -1, keepdims=True)).astype(jnp.bfloat16)
        values = jnp.concatenate(
            [near[0, 1, :, lanes], packed[2, :, lanes], near[1, 1, :, lanes]], axis=0
        )
        mixed[:, lanes] = jnp.dot(
            share, values, preferred_element_type=jnp.float32
        ).astype(jnp.bfloat16)

    for rows in range(2):
        project(me, rows, weight[rows * shard:(rows + 1) * shard])
    both(1, lambda zz, low: use(zz * COLS + x))
    use(across)
    for d in range(2, lines):
        both(d, take_line)
        both(d - 1, lambda zz, low: take_y(zz * COLS + x))
        if d == 2:
            take_y(across)
        both(d, lambda zz, low: use(zz * COLS + x))
    if lines > 1:
        both(lines - 1, lambda zz, low: take_y(zz * COLS + x))
    if lines < 3:
        take_y(across)
    for d in range(1, lines):
        both(d, take_across)
        both(d, lambda zz, low: use(zz * COLS + (1 - x)))
        if d > 1:
            both(d - 1, lambda zz, low: take_y(zz * COLS + (1 - x)))
    if lines > 1:
        both(lines - 1, lambda zz, low: take_y(zz * COLS + (1 - x)))

    square = jnp.zeros((count, 1), jnp.float32)
    for s in range(devices):
        for rows in range(2):
            sum_copy(s, rows).wait_recv()
            at = (2 * s + rows) * shard
            lanes = slice(at, at + shard)
            value = tokens[:, lanes].astype(jnp.float32) + (1.0 + modulation[0:1, lanes]) * (
                mine_out[s, rows] + their_out[s, rows]
            )
            state[:, lanes] = value
            square = square + jnp.sum(value * value, -1, keepdims=True)
    scale = lax.rsqrt(square / width + EPS)
    for s in range(2 * devices):
        lanes = slice(s * shard, (s + 1) * shard)
        normed[:, lanes] = (
            state[:, lanes] * scale * (1.0 + modulation[2:3, lanes]) + modulation[1:2, lanes]
        ).astype(jnp.bfloat16)
    logits = lax.dot_general(
        router[...], normed[...], (((1,), (1,)), ((), ())), preferred_element_type=jnp.float32
    )
    name = lax.broadcasted_iota(jnp.int32, logits.shape, 0)
    named = name == ids[0:1]
    for k in range(1, ids.shape[0]):
        named = named | (name == ids[k:k + 1])
    lifted = jnp.where(named, jax.nn.sigmoid(logits), 0.0)
    meta[...] = lifted / jnp.sum(lifted, 0, keepdims=True)

    for i in range(2):
        near_copy(i).wait_send()

        @pl.when(far_up | far_down)
        def _():
            far_copy(i, x_to).wait_send()

    @pl.when(not_top)
    def _():
        piece(me, 0, up_to, mine).wait_send()

    @pl.when(not_bottom)
    def _():
        piece(me, 1, down_to, mine).wait_send()

    piece(me, 2, x_to, mine).wait_send()
    piece(across, 3, y_to).wait_send()
    for d in range(1, lines):

        def sent(zz, low):
            s = zz * COLS + x

            @pl.when(not_top if low else not_bottom)
            def _():
                piece(s, 0 if low else 1, up_to).wait_send()

            piece(s, 2, x_to).wait_send()
            piece(s, 3, y_to).wait_send()
            piece(zz * COLS + (1 - x), 3, y_to).wait_send()

        both(d, sent)
    for s in range(devices):
        for rows in range(2):
            sum_copy(s, rows).wait_send()


def front_call(tokens, query_key_value, out_weight, modulation, router_weight, expert_ids):
    devices = lax.axis_size("dev")
    count, width = tokens.shape
    local = query_key_value.shape[2]
    shard = out_weight.shape[0] // 2
    lines = devices // COLS
    vmem = pl.BlockSpec(memory_space=pltpu.VMEM)
    dma = pltpu.SemaphoreType.DMA
    return pl.pallas_call(
        functools.partial(front_kernel, devices),
        out_shape=(
            jax.ShapeDtypeStruct((count, width), jnp.bfloat16),
            jax.ShapeDtypeStruct((count, width), jnp.float32),
            jax.ShapeDtypeStruct((router_weight.shape[1], count), jnp.float32),
        ),
        in_specs=[vmem] * 6,
        out_specs=(vmem, vmem, vmem),
        scratch_shapes=[
            pltpu.VMEM((2, 2, count, local), jnp.bfloat16),
            pltpu.VMEM((devices, 2, shard, local), jnp.bfloat16),
            pltpu.VMEM((count, local), jnp.bfloat16),
            pltpu.VMEM((devices, 2, count, shard), jnp.float32),
            pltpu.VMEM((devices, 2, count, shard), jnp.float32),
            dma((2,)), dma((2,)), dma((2,)), dma((2,)),
            dma((devices, 4)), dma((devices,)), dma((devices,)),
            dma((devices, 2)), dma((devices, 2)),
        ],
        compiler_params=pltpu.CompilerParams(
            collective_id=2, has_side_effects=True, vmem_limit_bytes=VMEM_BYTES // 2
        ),
    )(
        tokens, query_key_value.transpose(1, 0, 2), out_weight, modulation,
        router_weight.T, expert_ids.T,
    )


def expert_call(normed, meta, state, modulation, gate_up_weight, down_weight):
    devices = lax.axis_size("dev")
    count, width = normed.shape
    half = down_weight.shape[2]
    halves = gate_up_weight.shape[0]
    local = halves // 2
    gate_up_weight = gate_up_weight.swapaxes(2, 3)
    hidden = gate_up_weight.shape[2]
    lines = devices // COLS
    rows = devices * SLOT
    vmem = pl.BlockSpec(memory_space=pltpu.VMEM)
    hbm = pl.BlockSpec(memory_space=pl.ANY)
    dma = pltpu.SemaphoreType.DMA
    return pl.pallas_call(
        functools.partial(expert_kernel, devices),
        out_shape=jax.ShapeDtypeStruct((count, half), jnp.bfloat16),
        in_specs=[vmem, vmem, vmem, vmem, hbm, hbm],
        out_specs=vmem,
        scratch_shapes=[
            pltpu.VMEM((2, devices, count, half), jnp.bfloat16),
            pltpu.VMEM((2, local, rows, half), jnp.bfloat16),
            pltpu.VMEM(gate_up_weight.shape, jnp.bfloat16),
            pltpu.VMEM(down_weight.shape, jnp.bfloat16),
            pltpu.VMEM((halves, rows, hidden), jnp.bfloat16),
            pltpu.VMEM((halves, rows, hidden), jnp.bfloat16),
            pltpu.VMEM((devices, local, count), jnp.float32),
            pltpu.VMEM((devices, local * SLOT, count), jnp.bfloat16),
            pltpu.VMEM((local, rows, LANES), jnp.float32),
            pltpu.VMEM((lines, count, half), jnp.bfloat16),
            pltpu.VMEM((lines, count, half), jnp.bfloat16),
            pltpu.VMEM((lines, count, half), jnp.bfloat16),
            pltpu.VMEM((count, half), jnp.float32),
            dma((devices,)), dma((devices,)), dma((devices, 4)), dma((devices,)), dma((devices,)),
            dma((halves,)), dma((halves,)), dma((halves,)), dma((halves,)),
            dma((lines,)), dma((lines,)), dma((lines,)), dma((lines,)), dma((lines,)), dma((lines,)),
        ],
        compiler_params=pltpu.CompilerParams(
            collective_id=1, has_side_effects=True, vmem_limit_bytes=VMEM_BYTES
        ),
    )(normed, meta, state, modulation, gate_up_weight, down_weight)


def body(
    tokens,
    query_key_value,
    out_weight,
    modulation,
    router_weight,
    expert_ids,
    gate_up_weight,
    down_weight,
):
    count = tokens.shape[0]
    width = tokens.shape[1]
    parts = lax.axis_size("sub")
    part = lax.axis_index("sub")
    position = lax.axis_index("dev")
    devices = lax.axis_size("dev")
    total = count * devices
    local_width = query_key_value.shape[2]
    weight_bytes = 2 * (gate_up_weight.size + down_weight.size)
    token_bytes = 10 * devices * count * width
    fits = weight_bytes + token_bytes < VMEM_BYTES and CAP <= SLOT
    paired = parts == 2 and lax.axis_size("groups") == 2 and devices % COLS == 0
    tiled = out_weight.shape[0] % (2 * LANES) == 0 and count == LANES
    if fits and paired and tiled:
        normed, state, meta = front_call(
            tokens, query_key_value, out_weight, modulation, router_weight, expert_ids
        )
        return expert_call(normed, meta, state, modulation, gate_up_weight, down_weight)
    heads_here = local_width // HEAD
    query = query_key_value[:, 0].reshape(count, heads_here, HEAD)
    pair = query_key_value[:, 1:]
    near = extended(pair, (("dev", 0),), count)
    keys = near[:, 0].reshape(3 * count, heads_here, HEAD)
    values = near[:, 1].reshape(3 * count, heads_here, HEAD)
    mixed = window_attention(query, keys, values, position, total).reshape(count, local_width)
    partial_proj = lax.dot_general(
        mixed,
        lax.all_gather(out_weight, "dev", axis=0, tiled=True),
        (((1,), (1,)), ((), ())),
        preferred_element_type=jnp.float32,
    )
    proj = lax.psum(partial_proj, "sub")
    state = tokens.astype(jnp.float32) + (1.0 + modulation[0]) * proj
    normed = normalize(state, modulation)
    gates = route(normed, router_weight, expert_ids)
    experts = router_weight.shape[1]
    topk = expert_ids.shape[1]
    flat = expert_ids.reshape(-1)
    picks = flat.shape[0]
    onehot = (flat[:, None] == jnp.arange(experts, dtype=jnp.int32)[None, :]).astype(jnp.int32)
    rank = jnp.sum((jnp.cumsum(onehot, 0) - 1) * onehot, 1)
    target = flat * CAP + rank
    hit = target[None, :] == jnp.arange(experts * CAP, dtype=jnp.int32)[:, None]
    filled = jnp.any(hit, 1)
    anchor = jnp.sum(jnp.where(hit, jnp.arange(picks, dtype=jnp.int32)[None, :], 0), 1) // topk
    slice_width = width // parts
    sent = lax.dynamic_slice_in_dim(normed, part * slice_width, slice_width, 1)
    sent_width = sent.shape[1]
    rows_out = jnp.where(filled[:, None], sent[anchor], jnp.zeros((), jnp.bfloat16))
    halves_here = gate_up_weight.shape[0]
    doubled = jnp.broadcast_to(
        rows_out.reshape(experts, 1, CAP, sent_width), (experts, 2, CAP, sent_width)
    )
    outgoing = doubled.reshape(devices, halves_here, CAP, sent_width)
    up_form = "sxcd,xgdf->sxcgf"
    down_form = "sxcf,xfd->sxcd"
    incoming = lax.all_to_all(outgoing, "dev", split_axis=0, concat_axis=0, tiled=True)
    both = jnp.einsum(
        up_form,
        lax.all_gather(incoming, "sub", axis=3, tiled=True),
        gate_up_weight,
        preferred_element_type=jnp.float32,
    )
    hidden = (jax.nn.silu(both[..., 0, :]) * both[..., 1, :]).astype(jnp.bfloat16)
    gathered = lax.all_gather(hidden, "sub", axis=hidden.ndim - 1, tiled=True)
    result = jnp.einsum(down_form, gathered, down_weight, preferred_element_type=jnp.float32)
    returned = lax.all_to_all(
        result.astype(jnp.bfloat16), "dev", split_axis=0, concat_axis=0, tiled=True
    )
    own_width = returned.shape[-1]
    arranged = returned.reshape(experts, 2, CAP, own_width)
    answers = arranged[flat, :, rank, :].reshape(count, topk, 2, own_width).astype(jnp.float32)
    combined = answers[:, :, 0] + answers[:, :, 1]
    routed = jnp.einsum("tk,tkd->td", gates, combined)
    own = lax.dynamic_slice_in_dim(state, part * slice_width, slice_width, 1)
    lift = lax.dynamic_slice_in_dim(modulation[3], part * slice_width, slice_width, 0)
    return (own + (1.0 + lift) * routed).astype(jnp.bfloat16)


def solution(mesh):
    return jax.shard_map(
        body,
        mesh=mesh,
        in_specs=(
            P(("groups", "dev"), None),
            P(("groups", "dev"), None, "sub"),
            P("dev", "sub"),
            P("groups", None),
            P(),
            P(("groups", "dev"), None),
            P("dev", None, None, "sub"),
            P("dev", None, "sub"),
        ),
        out_specs=P(("groups", "dev"), "sub"),
        check_vma=False,
    )
```

```python
import functools
import math

import jax
import jax.numpy as jnp
from jax import lax
from jax.experimental import pallas as pl
from jax.experimental.pallas import tpu as pltpu
from jax.sharding import PartitionSpec as P

HEAD = 128
CAP = 12


EPS = 1e-06
NEG = -1e30


def extended(cells, sides, width):
    for axis, dim in sides:
        count = lax.axis_size(axis)
        ends = count - 1
        head = lax.slice_in_dim(cells, 0, width, axis=dim)
        tail = lax.slice_in_dim(cells, cells.shape[dim] - width, cells.shape[dim], axis=dim)
        cells = jnp.concatenate(
            [
                lax.ppermute(tail, axis, [(i, (i + 1) % count) for i in range(ends)]),
                cells,
                lax.ppermute(head, axis, [((i + 1) % count, i) for i in range(ends)]),
            ],
            axis=dim,
        )
    return cells


def window_attention(query, keys, values, index, total):
    count = query.shape[0]
    rows = jnp.arange(count, dtype=jnp.int32)[:, None]
    cols = jnp.arange(3 * count, dtype=jnp.int32)[None, :] - count
    place = index * count + cols
    allowed = (jnp.abs(cols - rows) <= count) & (place >= 0) & (place < total)
    scores = jnp.einsum(
        "qhd,khd->hqk", query, keys, preferred_element_type=jnp.float32
    ) / math.sqrt(query.shape[2])
    scores = jnp.where(allowed[None], scores, NEG)
    top = jnp.max(scores, -1, keepdims=True)
    weight = jnp.exp(scores - top)
    weight = (weight / jnp.sum(weight, -1, keepdims=True)).astype(jnp.bfloat16)
    mixed = jnp.einsum("hqk,khd->qhd", weight, values, preferred_element_type=jnp.float32)
    return mixed.astype(jnp.bfloat16)


def normalize(state, modulation):
    scale = lax.rsqrt(jnp.mean(state * state, -1, keepdims=True) + EPS)
    return (state * scale * (1.0 + modulation[2]) + modulation[1]).astype(jnp.bfloat16)


def route(normed, router_weight, expert_ids):
    logits = jnp.dot(normed, router_weight, preferred_element_type=jnp.float32)
    experts = router_weight.shape[1]
    match = expert_ids[:, :, None] == jnp.arange(experts, dtype=jnp.int32)[None, None, :]
    picked = jnp.sum(jnp.where(match, logits[:, None, :], 0.0), -1)
    lifted = jax.nn.sigmoid(picked)
    return lifted / jnp.sum(lifted, -1, keepdims=True)


LANES = 128
SLOT = 16
COLS = 2
VMEM_BYTES = 66 * 1000 * 1000
MESH = pl.DeviceIdType.MESH


def expert_kernel(
    devices, weight_copies,
    normed, meta, state, modulation, gate_up, down,
    out,
    tok, disp, gu, dn, hid_own, hid_other, got_meta, pick, slot_gate, got_x, got_up, got_down, acc,
    meta_s, meta_r, ag_s, ag_r, core_r, hid_s, hid_r,
    x_s, x_r, up_s, up_r, down_s, down_r,
):
    me = lax.axis_index("dev")
    part = lax.axis_index("sub")
    other = 1 - part
    z = me // COLS
    x = me % COLS
    across = z * COLS + (1 - x)
    lines = devices // COLS
    count, width = normed.shape
    half = width // 2
    halves = gate_up.shape[0]
    local = halves // 2
    hidden = gate_up.shape[2]
    slots = local * SLOT

    def remote(src, dst, send, recv, where):
        return pltpu.make_async_remote_copy(
            src_ref=src, dst_ref=dst, send_sem=send, recv_sem=recv,
            device_id=where, device_id_type=MESH,
        )

    def block(s, way, where, src=None):
        dst = tok.at[part, s]
        recv = core_r.at[s] if way == 3 else ag_r.at[s]
        return remote(dst if src is None else src, dst, ag_s.at[s, way], recv, where)

    up_to = {"dev": jnp.minimum(me + COLS, devices - 1)}
    down_to = {"dev": jnp.maximum(me - COLS, 0)}
    x_to = {"dev": across}
    core_to = {"sub": other}
    not_top = z < lines - 1
    not_bottom = z > 0
    mine = normed.at[:, pl.ds(pl.multiple_of(part * half, LANES), half)]

    def meta_copy(step):
        target = (me + step) % devices
        return remote(
            meta.at[pl.ds(pl.multiple_of(target * local, local), local)], got_meta.at[me],
            meta_s.at[step - 1], meta_r.at[me], {"dev": target},
        )

    for step in range(1, devices):
        meta_copy(step).start()

    @pl.when(not_top)
    def _():
        block(me, 0, up_to, mine).start()

    @pl.when(not_bottom)
    def _():
        block(me, 1, down_to, mine).start()

    block(me, 2, x_to, mine).start()

    before = (
        lax.broadcasted_iota(jnp.int32, (count, count), 0)
        < lax.broadcasted_iota(jnp.int32, (count, count), 1)
    ).astype(jnp.float32).astype(jnp.bfloat16)
    place = lax.broadcasted_iota(jnp.int32, (local, SLOT, count), 1).astype(jnp.float32)

    def routing(s, gate):
        chosen = jnp.where(gate > 0.0, 1.0, 0.0)
        rank = jnp.dot(chosen.astype(jnp.bfloat16), before, preferred_element_type=jnp.float32)
        rank = jnp.where(gate > 0.0, rank, -1.0)
        hit = jnp.broadcast_to(rank[:, None, :], place.shape) == place
        pick[s] = jnp.where(hit, 1.0, 0.0).reshape(slots, count).astype(jnp.bfloat16)
        value = jnp.where(hit, jnp.broadcast_to(gate[:, None, :], place.shape), 0.0)
        value = jnp.sum(value, -1, keepdims=True)
        slot_gate[:, pl.ds(pl.multiple_of(s * SLOT, SLOT), SLOT), :] = jnp.broadcast_to(
            value, (local, SLOT, LANES)
        )

    def dispatch(s, h, rows):
        moved = jnp.dot(pick[s], rows, preferred_element_type=jnp.float32)
        disp[h, :, pl.ds(pl.multiple_of(s * SLOT, SLOT), SLOT), :] = moved.astype(
            jnp.bfloat16
        ).reshape(local, SLOT, half)

    routing(me, meta[pl.ds(pl.multiple_of(me * local, local), local)])
    dispatch(me, 0, normed[:, :half])
    dispatch(me, 1, normed[:, half:])
    for step in range(1, devices):
        s = (me + step) % devices
        remote(
            meta.at[pl.ds(0, local)], got_meta.at[s], meta_s.at[0], meta_r.at[s], {"dev": s}
        ).wait_recv()
        routing(s, got_meta[s])

    def arrive(s):
        block(s, 2, x_to).wait_recv()

    def from_line(zz, way, where, more):
        s = zz * COLS + x
        arrive(s)

        @pl.when(more)
        def _():
            block(s, way, where).start()

        block(s, 2, x_to).start()
        block(s, 3, core_to).start()
        dispatch(s, part, tok[part, s])

    def from_across(zz):
        s = zz * COLS + (1 - x)
        arrive(s)
        block(s, 3, core_to).start()
        dispatch(s, part, tok[part, s])

    def from_core(s):
        remote(tok.at[other, s], tok.at[other, s], ag_s.at[s, 3], core_r.at[s], core_to).wait_recv()
        dispatch(s, other, tok[other, s])

    def both(d, act):
        @pl.when(z - d >= 0)
        def _():
            act(z - d, True)

        @pl.when(z + d < lines)
        def _():
            act(z + d, False)

    for d in range(1, lines):
        both(d, lambda zz, low: from_line(
            zz, 0 if low else 1, up_to if low else down_to, not_top if low else not_bottom
        ))
        if d == 1:
            from_across(z)
        else:
            both(d - 1, lambda zz, low: from_core(zz * COLS + x))
    both(lines - 1, lambda zz, low: from_core(zz * COLS + x))
    from_core(across)
    for d in range(1, lines):
        both(d, lambda zz, low: from_across(zz))
        if d > 1:
            both(d - 1, lambda zz, low: from_core(zz * COLS + (1 - x)))
    both(lines - 1, lambda zz, low: from_core(zz * COLS + (1 - x)))

    @pl.when(not_top)
    def _():
        block(me, 0, up_to, mine).wait_send()

    @pl.when(not_bottom)
    def _():
        block(me, 1, down_to, mine).wait_send()

    block(me, 2, x_to, mine).wait_send()
    for d in range(1, lines):

        def sent(zz, low):
            s = zz * COLS + x

            @pl.when(not_top if low else not_bottom)
            def _():
                block(s, 0 if low else 1, up_to).wait_send()

            block(s, 2, x_to).wait_send()
            block(s, 3, core_to).wait_send()
            block(zz * COLS + (1 - x), 3, core_to).wait_send()

        both(d, sent)
    block(across, 3, core_to).wait_send()

    def hid_copy(h):
        return remote(hid_own.at[h], hid_other.at[h], hid_s.at[h], hid_r.at[h], core_to)

    def across_rows(left, right):
        return lax.dot_general(
            left, right, (((1,), (1,)), ((), ())), preferred_element_type=jnp.float32
        )

    def raise_expert(e):
        low, high = disp[0, e], disp[1, e]
        for b in range(2):
            h = 2 * e + b
            weight_copies(h)[0].wait()

            def product(g):
                return across_rows(low, gu[h, g, :, :half]) + across_rows(high, gu[h, g, :, half:])

            gate = product(0)
            hid_own[h] = (gate * jax.nn.sigmoid(gate) * product(1)).astype(jnp.bfloat16)
            hid_copy(h).start()

    def lower_expert(e):
        total = None
        for b in range(2):
            h = 2 * e + b
            weight_copies(h)[1].wait()
            hid_copy(h).wait_recv()
            first = dn[h, pl.ds(pl.multiple_of(part * hidden, SLOT), hidden), :]
            second = dn[h, pl.ds(pl.multiple_of(other * hidden, SLOT), hidden), :]
            piece = jnp.dot(hid_own[h], first, preferred_element_type=jnp.float32) + jnp.dot(
                hid_other[h], second, preferred_element_type=jnp.float32
            )
            piece = piece.astype(jnp.bfloat16).astype(jnp.float32)
            total = piece if total is None else total + piece
        gain = slot_gate[e][:, :1]
        disp[0, e] = (total * gain).astype(jnp.bfloat16)

    raise_expert(0)

    def step_expert(e, carry):
        raise_expert(e)
        lower_expert(e - 1)
        return carry

    lax.fori_loop(1, local, step_expert, 0)
    lower_expert(local - 1)

    def combine(s):
        rows = disp[0, :, pl.ds(pl.multiple_of(s * SLOT, SLOT), SLOT), :].reshape(slots, half)
        return lax.dot_general(
            pick[s], rows, (((0,), (0,)), ((), ())), preferred_element_type=jnp.float32
        )

    def x_copy(zz):
        return remote(
            tok.at[0, zz * COLS + (1 - x)], got_x.at[zz], x_s.at[zz], x_r.at[zz], x_to
        )

    def line_copy(zz, low):
        if low:
            return remote(tok.at[1, zz], got_down.at[zz], down_s.at[zz], down_r.at[zz], down_to)
        return remote(tok.at[1, zz], got_up.at[zz], up_s.at[zz], up_r.at[zz], up_to)

    def give_across(zz, low):
        s = zz * COLS + (1 - x)
        tok[0, s] = combine(s).astype(jnp.bfloat16)
        x_copy(zz).start()

    def add_line(zz, low):
        line_copy(zz, low).wait_recv()
        acc[...] += (got_down if low else got_up)[zz].astype(jnp.float32)

    def gather_here(zz):
        acc[...] = combine(zz * COLS + x)
        x_copy(zz).wait_recv()
        acc[...] += got_x[zz].astype(jnp.float32)

    def pass_on(zz, low):
        gather_here(zz)

        @pl.when(not_top if low else not_bottom)
        def _():
            add_line(zz, low)

        tok[1, zz] = acc[...].astype(jnp.bfloat16)
        line_copy(zz, low).start()

    for d in range(lines - 1, 0, -1):
        both(d, give_across)
    give_across(z, False)
    for d in range(lines - 1, 0, -1):
        both(d, pass_on)
    gather_here(z)

    @pl.when(not_bottom)
    def _():
        add_line(z, False)

    @pl.when(not_top)
    def _():
        add_line(z, True)

    own = pl.ds(pl.multiple_of(part * half, LANES), half)
    out[...] = (state[:, own] + (1.0 + modulation[3:4, own]) * acc[...]).astype(out.dtype)

    for d in range(1, lines):

        def drained(zz, low):
            line_copy(zz, low).wait_send()
            x_copy(zz).wait_send()

        both(d, drained)
    x_copy(z).wait_send()
    for step in range(1, devices):
        meta_copy(step).wait_send()

    def hid_drain(h, carry):
        hid_copy(h).wait_send()
        return carry

    lax.fori_loop(0, halves, hid_drain, 0)


def front_kernel(
    devices, start_weights,
    sources, held, own_sem,
    normed, state, meta,
    near, wide, mixed, mine_out, their_out,
    near_s, near_r, far_s, far_r, ag_s, ag_r, y_r, sum_s, sum_r,
):
    packed_hbm, weight_hbm = sources[1], sources[2]
    tokens, packed, weight, modulation, router, ids = held

    def own_copy(i):
        return pltpu.make_async_copy(sources[i], held[i], own_sem.at[i])

    for i in (1, 2, 0, 3, 4, 5):
        own_copy(i).start()
    me = lax.axis_index("dev")
    part = lax.axis_index("sub")
    group = lax.axis_index("groups")
    z = me // COLS
    x = me % COLS
    across = z * COLS + (1 - x)
    lines = devices // COLS
    count, width = tokens.shape
    shard = weight.shape[0] // 2
    not_top = z < lines - 1
    not_bottom = z > 0
    up_to = {"dev": jnp.minimum(me + COLS, devices - 1)}
    down_to = {"dev": jnp.maximum(me - COLS, 0)}
    x_to = {"dev": across}
    y_to = {"groups": 1 - group}
    core_to = {"sub": 1 - part}

    barrier = pltpu.get_barrier_semaphore()
    for step in range(1, devices):
        pl.semaphore_signal(
            barrier, inc=1, device_id={"dev": (me + step) % devices}, device_id_type=MESH
        )
    pl.semaphore_signal(barrier, inc=1, device_id=core_to, device_id_type=MESH)
    pl.semaphore_signal(barrier, inc=1, device_id=y_to, device_id_type=MESH)
    pl.semaphore_wait(barrier, devices + 1)

    def remote(src, dst, send, recv, where):
        return pltpu.make_async_remote_copy(
            src_ref=src, dst_ref=dst, send_sem=send, recv_sem=recv,
            device_id=where, device_id_type=MESH,
        )

    def near_copy(i):
        return remote(packed_hbm.at[1 + i], near.at[x, i], near_s.at[i], near_r.at[i], x_to)

    def far_copy(i, where):
        return remote(near.at[1 - x, i], near.at[x, i], far_s.at[i], far_r.at[i], where)

    def piece(s, way, where, src=None):
        dst = wide.at[s, group]
        recv = y_r.at[s] if way == 3 else ag_r.at[s]
        return remote(dst if src is None else src, dst, ag_s.at[s, way], recv, where)

    far_up = (x == 0) & not_top
    far_down = (x == 1) & not_bottom
    have_far = ((x == 0) & not_bottom) | ((x == 1) & not_top)
    mine = weight_hbm.at[pl.ds(pl.multiple_of(group * shard, SLOT), shard)]

    for i in range(2):
        near_copy(i).start()

    @pl.when(not_top)
    def _():
        piece(me, 0, up_to, mine).start()

    @pl.when(not_bottom)
    def _():
        piece(me, 1, down_to, mine).start()

    piece(me, 2, x_to, mine).start()
    start_weights()

    @pl.when(jnp.logical_not(have_far))
    def _():
        near[x] = jnp.zeros_like(near[x])

    for i in range(2):
        near_copy(i).wait_recv()

        @pl.when(far_up)
        def _():
            far_copy(i, up_to).start()

        @pl.when(far_down)
        def _():
            far_copy(i, down_to).start()

    def both(d, act):
        @pl.when(z - d >= 0)
        def _():
            act(z - d, True)

        @pl.when(z + d < lines)
        def _():
            act(z + d, False)

    def project(s, rows, block):
        mine_out[s, rows] = lax.dot_general(
            mixed[...], block, (((1,), (1,)), ((), ())), preferred_element_type=jnp.float32
        )
        sum_copy(s, rows).start()

    def sum_copy(s, rows):
        return remote(
            mine_out.at[s, rows], their_out.at[s, rows], sum_s.at[s, rows], sum_r.at[s, rows], core_to
        )

    def take_line(zz, low):
        s = zz * COLS + x
        piece(s, 2, x_to).wait_recv()

        @pl.when(not_top if low else not_bottom)
        def _():
            piece(s, 0 if low else 1, up_to if low else down_to).start()

        piece(s, 2, x_to).start()
        piece(s, 3, y_to).start()

    def take_across(zz, low):
        s = zz * COLS + (1 - x)
        piece(s, 2, x_to).wait_recv()
        piece(s, 3, y_to).start()

    def take_y(s):
        dst = wide.at[s, 1 - group]
        remote(dst, dst, ag_s.at[s, 3], y_r.at[s], y_to).wait_recv()
        project(s, 1 - group, wide[s, 1 - group])

    def use(s):
        project(s, group, wide[s, group])

    both(1, take_line)
    take_across(z, False)
    for i in range(6):
        own_copy(i).wait()

    @pl.when(have_far)
    def _():
        for i in range(2):
            far_copy(i, x_to).wait_recv()

    row = lax.broadcasted_iota(jnp.int32, (count, count), 0)
    col = lax.broadcasted_iota(jnp.int32, (count, count), 1)
    see_before = (col >= row) & (me > 0)
    see_after = (col <= row) & (me < devices - 1)
    for h in range(mixed.shape[1] // HEAD):
        lanes = slice(h * HEAD, (h + 1) * HEAD)
        query = packed[0, :, lanes]

        def score(keys):
            return lax.dot_general(
                query, keys, (((1,), (1,)), ((), ())), preferred_element_type=jnp.float32
            ) / math.sqrt(HEAD)

        scores = jnp.concatenate(
            [
                jnp.where(see_before, score(near[0, 0, :, lanes]), NEG),
                score(packed[1, :, lanes]),
                jnp.where(see_after, score(near[1, 0, :, lanes]), NEG),
            ],
            axis=1,
        )
        top = jnp.max(scores, -1, keepdims=True)
        share = jnp.exp(scores - top)
        share = (share / jnp.sum(share, -1, keepdims=True)).astype(jnp.bfloat16)
        values = jnp.concatenate(
            [near[0, 1, :, lanes], packed[2, :, lanes], near[1, 1, :, lanes]], axis=0
        )
        mixed[:, lanes] = jnp.dot(
            share, values, preferred_element_type=jnp.float32
        ).astype(jnp.bfloat16)

    for rows in range(2):
        project(me, rows, weight[rows * shard:(rows + 1) * shard])
    both(1, lambda zz, low: use(zz * COLS + x))
    use(across)
    for d in range(2, lines):
        both(d, take_line)
        both(d - 1, lambda zz, low: take_y(zz * COLS + x))
        if d == 2:
            take_y(across)
        both(d, lambda zz, low: use(zz * COLS + x))
    if lines > 1:
        both(lines - 1, lambda zz, low: take_y(zz * COLS + x))
    if lines < 3:
        take_y(across)
    for d in range(1, lines):
        both(d, take_across)
        both(d, lambda zz, low: use(zz * COLS + (1 - x)))
        if d > 1:
            both(d - 1, lambda zz, low: take_y(zz * COLS + (1 - x)))
    if lines > 1:
        both(lines - 1, lambda zz, low: take_y(zz * COLS + (1 - x)))

    square = jnp.zeros((count, 1), jnp.float32)
    for s in range(devices):
        for rows in range(2):
            sum_copy(s, rows).wait_recv()
            at = (2 * s + rows) * shard
            lanes = slice(at, at + shard)
            value = tokens[:, lanes].astype(jnp.float32) + (1.0 + modulation[0:1, lanes]) * (
                mine_out[s, rows] + their_out[s, rows]
            )
            state[:, lanes] = value
            square = square + jnp.sum(value * value, -1, keepdims=True)
    scale = lax.rsqrt(square / width + EPS)
    for s in range(2 * devices):
        lanes = slice(s * shard, (s + 1) * shard)
        normed[:, lanes] = (
            state[:, lanes] * scale * (1.0 + modulation[2:3, lanes]) + modulation[1:2, lanes]
        ).astype(jnp.bfloat16)
    logits = lax.dot_general(
        router[...], normed[...], (((1,), (1,)), ((), ())), preferred_element_type=jnp.float32
    )
    name = lax.broadcasted_iota(jnp.int32, logits.shape, 0)
    named = name == ids[0:1]
    for k in range(1, ids.shape[0]):
        named = named | (name == ids[k:k + 1])
    lifted = jnp.where(named, jax.nn.sigmoid(logits), 0.0)
    meta[...] = lifted / jnp.sum(lifted, 0, keepdims=True)

    for i in range(2):
        near_copy(i).wait_send()

        @pl.when(far_up | far_down)
        def _():
            far_copy(i, x_to).wait_send()

    @pl.when(not_top)
    def _():
        piece(me, 0, up_to, mine).wait_send()

    @pl.when(not_bottom)
    def _():
        piece(me, 1, down_to, mine).wait_send()

    piece(me, 2, x_to, mine).wait_send()
    piece(across, 3, y_to).wait_send()
    for d in range(1, lines):

        def sent(zz, low):
            s = zz * COLS + x

            @pl.when(not_top if low else not_bottom)
            def _():
                piece(s, 0 if low else 1, up_to).wait_send()

            piece(s, 2, x_to).wait_send()
            piece(s, 3, y_to).wait_send()
            piece(zz * COLS + (1 - x), 3, y_to).wait_send()

        both(d, sent)
    for s in range(devices):
        for rows in range(2):
            sum_copy(s, rows).wait_send()


def block_kernel(devices, *refs):
    sources, gate_up, down, out = refs[:6], refs[6], refs[7], refs[8]
    held, normed, state, meta = refs[9:15], refs[15], refs[16], refs[17]
    front_buffers, expert_buffers = refs[18:23], refs[23:36]
    own_sem, gu_sem, dn_sem = refs[36:39]
    front_sems, expert_sems = refs[39:48], refs[48:]
    gu, dn = expert_buffers[2:4]
    halves = gate_up.shape[0]

    def weight_copies(h):
        return (
            pltpu.make_async_copy(gate_up.at[h], gu.at[h], gu_sem.at[h]),
            pltpu.make_async_copy(down.at[h], dn.at[h], dn_sem.at[h]),
        )

    def start_weights():
        def one(h, carry):
            for copy in weight_copies(h):
                copy.start()
            return carry

        lax.fori_loop(0, halves, one, 0)

    front_kernel(
        devices, start_weights, sources, held, own_sem, normed, state, meta,
        *front_buffers, *front_sems,
    )
    expert_kernel(
        devices, weight_copies, normed, meta, state, held[3], gate_up, down, out,
        *expert_buffers, *expert_sems,
    )


def block_call(
    tokens, query_key_value, out_weight, modulation, router_weight, expert_ids,
    gate_up_weight, down_weight,
):
    devices = lax.axis_size("dev")
    count, width = tokens.shape
    half = down_weight.shape[2]
    halves = gate_up_weight.shape[0]
    local = halves // 2
    gate_up_weight = gate_up_weight.swapaxes(2, 3)
    hidden = gate_up_weight.shape[2]
    lines = devices // COLS
    rows = devices * SLOT
    shard = out_weight.shape[0] // 2
    own = (
        tokens, query_key_value.transpose(1, 0, 2), out_weight, modulation,
        router_weight.T, expert_ids.T,
    )
    hbm = pl.BlockSpec(memory_space=pl.ANY)
    dma = pltpu.SemaphoreType.DMA
    return pl.pallas_call(
        functools.partial(block_kernel, devices),
        out_shape=jax.ShapeDtypeStruct((count, half), jnp.bfloat16),
        in_specs=[hbm] * 8,
        out_specs=pl.BlockSpec(memory_space=pltpu.VMEM),
        scratch_shapes=[
            *[pltpu.VMEM(array.shape, array.dtype) for array in own],
            pltpu.VMEM((count, width), jnp.bfloat16),
            pltpu.VMEM((count, width), jnp.float32),
            pltpu.VMEM((router_weight.shape[1], count), jnp.float32),
            pltpu.VMEM((2, 2, count, half), jnp.bfloat16),
            pltpu.VMEM((devices, 2, shard, half), jnp.bfloat16),
            pltpu.VMEM((count, half), jnp.bfloat16),
            pltpu.VMEM((devices, 2, count, shard), jnp.float32),
            pltpu.VMEM((devices, 2, count, shard), jnp.float32),
            pltpu.VMEM((2, devices, count, half), jnp.bfloat16),
            pltpu.VMEM((2, local, rows, half), jnp.bfloat16),
            pltpu.VMEM(gate_up_weight.shape, jnp.bfloat16),
            pltpu.VMEM(down_weight.shape, jnp.bfloat16),
            pltpu.VMEM((halves, rows, hidden), jnp.bfloat16),
            pltpu.VMEM((halves, rows, hidden), jnp.bfloat16),
            pltpu.VMEM((devices, local, count), jnp.float32),
            pltpu.VMEM((devices, local * SLOT, count), jnp.bfloat16),
            pltpu.VMEM((local, rows, LANES), jnp.float32),
            pltpu.VMEM((lines, count, half), jnp.bfloat16),
            pltpu.VMEM((lines, count, half), jnp.bfloat16),
            pltpu.VMEM((lines, count, half), jnp.bfloat16),
            pltpu.VMEM((count, half), jnp.float32),
            dma((6,)), dma((halves,)), dma((halves,)),
            dma((2,)), dma((2,)), dma((2,)), dma((2,)),
            dma((devices, 4)), dma((devices,)), dma((devices,)),
            dma((devices, 2)), dma((devices, 2)),
            dma((devices,)), dma((devices,)), dma((devices, 4)), dma((devices,)), dma((devices,)),
            dma((halves,)), dma((halves,)),
            dma((lines,)), dma((lines,)), dma((lines,)), dma((lines,)), dma((lines,)), dma((lines,)),
        ],
        compiler_params=pltpu.CompilerParams(
            collective_id=1, has_side_effects=True, vmem_limit_bytes=VMEM_BYTES
        ),
    )(*own, gate_up_weight, down_weight)


def body(
    tokens,
    query_key_value,
    out_weight,
    modulation,
    router_weight,
    expert_ids,
    gate_up_weight,
    down_weight,
):
    count = tokens.shape[0]
    width = tokens.shape[1]
    parts = lax.axis_size("sub")
    part = lax.axis_index("sub")
    position = lax.axis_index("dev")
    devices = lax.axis_size("dev")
    total = count * devices
    local_width = query_key_value.shape[2]
    weight_bytes = 2 * (gate_up_weight.size + down_weight.size)
    token_bytes = 12 * devices * count * width
    fits = weight_bytes + token_bytes < VMEM_BYTES and CAP <= SLOT
    paired = parts == 2 and lax.axis_size("groups") == 2 and devices % COLS == 0
    tiled = out_weight.shape[0] % (2 * LANES) == 0 and count == LANES
    if fits and paired and tiled:
        return block_call(
            tokens, query_key_value, out_weight, modulation, router_weight, expert_ids,
            gate_up_weight, down_weight,
        )
    heads_here = local_width // HEAD
    query = query_key_value[:, 0].reshape(count, heads_here, HEAD)
    pair = query_key_value[:, 1:]
    near = extended(pair, (("dev", 0),), count)
    keys = near[:, 0].reshape(3 * count, heads_here, HEAD)
    values = near[:, 1].reshape(3 * count, heads_here, HEAD)
    mixed = window_attention(query, keys, values, position, total).reshape(count, local_width)
    partial_proj = lax.dot_general(
        mixed,
        lax.all_gather(out_weight, "dev", axis=0, tiled=True),
        (((1,), (1,)), ((), ())),
        preferred_element_type=jnp.float32,
    )
    proj = lax.psum(partial_proj, "sub")
    state = tokens.astype(jnp.float32) + (1.0 + modulation[0]) * proj
    normed = normalize(state, modulation)
    gates = route(normed, router_weight, expert_ids)
    experts = router_weight.shape[1]
    topk = expert_ids.shape[1]
    flat = expert_ids.reshape(-1)
    picks = flat.shape[0]
    onehot = (flat[:, None] == jnp.arange(experts, dtype=jnp.int32)[None, :]).astype(jnp.int32)
    rank = jnp.sum((jnp.cumsum(onehot, 0) - 1) * onehot, 1)
    target = flat * CAP + rank
    hit = target[None, :] == jnp.arange(experts * CAP, dtype=jnp.int32)[:, None]
    filled = jnp.any(hit, 1)
    anchor = jnp.sum(jnp.where(hit, jnp.arange(picks, dtype=jnp.int32)[None, :], 0), 1) // topk
    slice_width = width // parts
    sent = lax.dynamic_slice_in_dim(normed, part * slice_width, slice_width, 1)
    sent_width = sent.shape[1]
    rows_out = jnp.where(filled[:, None], sent[anchor], jnp.zeros((), jnp.bfloat16))
    halves_here = gate_up_weight.shape[0]
    doubled = jnp.broadcast_to(
        rows_out.reshape(experts, 1, CAP, sent_width), (experts, 2, CAP, sent_width)
    )
    outgoing = doubled.reshape(devices, halves_here, CAP, sent_width)
    up_form = "sxcd,xgdf->sxcgf"
    down_form = "sxcf,xfd->sxcd"
    incoming = lax.all_to_all(outgoing, "dev", split_axis=0, concat_axis=0, tiled=True)
    both = jnp.einsum(
        up_form,
        lax.all_gather(incoming, "sub", axis=3, tiled=True),
        gate_up_weight,
        preferred_element_type=jnp.float32,
    )
    hidden = (jax.nn.silu(both[..., 0, :]) * both[..., 1, :]).astype(jnp.bfloat16)
    gathered = lax.all_gather(hidden, "sub", axis=hidden.ndim - 1, tiled=True)
    result = jnp.einsum(down_form, gathered, down_weight, preferred_element_type=jnp.float32)
    returned = lax.all_to_all(
        result.astype(jnp.bfloat16), "dev", split_axis=0, concat_axis=0, tiled=True
    )
    own_width = returned.shape[-1]
    arranged = returned.reshape(experts, 2, CAP, own_width)
    answers = arranged[flat, :, rank, :].reshape(count, topk, 2, own_width).astype(jnp.float32)
    combined = answers[:, :, 0] + answers[:, :, 1]
    routed = jnp.einsum("tk,tkd->td", gates, combined)
    own = lax.dynamic_slice_in_dim(state, part * slice_width, slice_width, 1)
    lift = lax.dynamic_slice_in_dim(modulation[3], part * slice_width, slice_width, 0)
    return (own + (1.0 + lift) * routed).astype(jnp.bfloat16)


def solution(mesh):
    return jax.shard_map(
        body,
        mesh=mesh,
        in_specs=(
            P(("groups", "dev"), None),
            P(("groups", "dev"), None, "sub"),
            P("dev", "sub"),
            P("groups", None),
            P(),
            P(("groups", "dev"), None),
            P("dev", None, None, "sub"),
            P("dev", None, "sub"),
        ),
        out_specs=P(("groups", "dev"), "sub"),
        check_vma=False,
    )
```

```python
import functools
import math

import jax
import jax.numpy as jnp
from jax import lax
from jax.experimental import pallas as pl
from jax.experimental.pallas import tpu as pltpu
from jax.sharding import PartitionSpec as P

HEAD = 128
CAP = 12


EPS = 1e-06
NEG = -1e30


def extended(cells, sides, width):
    for axis, dim in sides:
        count = lax.axis_size(axis)
        ends = count - 1
        head = lax.slice_in_dim(cells, 0, width, axis=dim)
        tail = lax.slice_in_dim(cells, cells.shape[dim] - width, cells.shape[dim], axis=dim)
        cells = jnp.concatenate(
            [
                lax.ppermute(tail, axis, [(i, (i + 1) % count) for i in range(ends)]),
                cells,
                lax.ppermute(head, axis, [((i + 1) % count, i) for i in range(ends)]),
            ],
            axis=dim,
        )
    return cells


def window_attention(query, keys, values, index, total):
    count = query.shape[0]
    rows = jnp.arange(count, dtype=jnp.int32)[:, None]
    cols = jnp.arange(3 * count, dtype=jnp.int32)[None, :] - count
    place = index * count + cols
    allowed = (jnp.abs(cols - rows) <= count) & (place >= 0) & (place < total)
    scores = jnp.einsum(
        "qhd,khd->hqk", query, keys, preferred_element_type=jnp.float32
    ) / math.sqrt(query.shape[2])
    scores = jnp.where(allowed[None], scores, NEG)
    top = jnp.max(scores, -1, keepdims=True)
    weight = jnp.exp(scores - top)
    weight = (weight / jnp.sum(weight, -1, keepdims=True)).astype(jnp.bfloat16)
    mixed = jnp.einsum("hqk,khd->qhd", weight, values, preferred_element_type=jnp.float32)
    return mixed.astype(jnp.bfloat16)


def normalize(state, modulation):
    scale = lax.rsqrt(jnp.mean(state * state, -1, keepdims=True) + EPS)
    return (state * scale * (1.0 + modulation[2]) + modulation[1]).astype(jnp.bfloat16)


def route(normed, router_weight, expert_ids):
    logits = jnp.dot(normed, router_weight, preferred_element_type=jnp.float32)
    experts = router_weight.shape[1]
    match = expert_ids[:, :, None] == jnp.arange(experts, dtype=jnp.int32)[None, None, :]
    picked = jnp.sum(jnp.where(match, logits[:, None, :], 0.0), -1)
    lifted = jax.nn.sigmoid(picked)
    return lifted / jnp.sum(lifted, -1, keepdims=True)


LANES = 128
SLOT = 16
COLS = 2
VMEM_BYTES = 66 * 1000 * 1000
MESH = pl.DeviceIdType.MESH


def expert_kernel(
    devices, weight_copies,
    normed, meta, state, modulation, gate_up, down,
    out,
    tok, disp, gu, dn, hid_own, hid_other, got_meta, pick, slot_gate, got_x, got_up, got_down, acc,
    meta_s, meta_r, ag_s, ag_r, core_r, hid_s, hid_r,
    x_s, x_r, up_s, up_r, down_s, down_r,
):
    me = lax.axis_index("dev")
    part = lax.axis_index("sub")
    other = 1 - part
    z = me // COLS
    x = me % COLS
    across = z * COLS + (1 - x)
    lines = devices // COLS
    count, width = normed.shape
    half = width // 2
    halves = gate_up.shape[0]
    local = halves // 2
    hidden = gate_up.shape[2]
    slots = local * SLOT

    def remote(src, dst, send, recv, where):
        return pltpu.make_async_remote_copy(
            src_ref=src, dst_ref=dst, send_sem=send, recv_sem=recv,
            device_id=where, device_id_type=MESH,
        )

    def block(s, way, where, src=None):
        dst = tok.at[part, s]
        recv = core_r.at[s] if way == 3 else ag_r.at[s]
        return remote(dst if src is None else src, dst, ag_s.at[s, way], recv, where)

    up_to = {"dev": jnp.minimum(me + COLS, devices - 1)}
    down_to = {"dev": jnp.maximum(me - COLS, 0)}
    x_to = {"dev": across}
    core_to = {"sub": other}
    not_top = z < lines - 1
    not_bottom = z > 0
    mine = normed.at[:, pl.ds(pl.multiple_of(part * half, LANES), half)]

    def meta_copy(step):
        target = (me + step) % devices
        return remote(
            meta.at[pl.ds(pl.multiple_of(target * local, local), local)], got_meta.at[me],
            meta_s.at[step - 1], meta_r.at[me], {"dev": target},
        )

    for step in range(1, devices):
        meta_copy(step).start()

    @pl.when(not_top)
    def _():
        block(me, 0, up_to, mine).start()

    @pl.when(not_bottom)
    def _():
        block(me, 1, down_to, mine).start()

    block(me, 2, x_to, mine).start()

    before = (
        lax.broadcasted_iota(jnp.int32, (count, count), 0)
        < lax.broadcasted_iota(jnp.int32, (count, count), 1)
    ).astype(jnp.float32).astype(jnp.bfloat16)
    place = lax.broadcasted_iota(jnp.int32, (local, SLOT, count), 1).astype(jnp.float32)

    def routing(s, gate):
        chosen = jnp.where(gate > 0.0, 1.0, 0.0)
        rank = jnp.dot(chosen.astype(jnp.bfloat16), before, preferred_element_type=jnp.float32)
        rank = jnp.where(gate > 0.0, rank, -1.0)
        hit = jnp.broadcast_to(rank[:, None, :], place.shape) == place
        pick[s] = jnp.where(hit, 1.0, 0.0).reshape(slots, count).astype(jnp.bfloat16)
        value = jnp.where(hit, jnp.broadcast_to(gate[:, None, :], place.shape), 0.0)
        value = jnp.sum(value, -1, keepdims=True)
        slot_gate[:, pl.ds(pl.multiple_of(s * SLOT, SLOT), SLOT), :] = jnp.broadcast_to(
            value, (local, SLOT, LANES)
        )

    def dispatch(s, h, rows):
        moved = jnp.dot(pick[s], rows, preferred_element_type=jnp.float32)
        disp[h, :, pl.ds(pl.multiple_of(s * SLOT, SLOT), SLOT), :] = moved.astype(
            jnp.bfloat16
        ).reshape(local, SLOT, half)

    routing(me, meta[pl.ds(pl.multiple_of(me * local, local), local)])
    dispatch(me, 0, normed[:, :half])
    dispatch(me, 1, normed[:, half:])
    for step in range(1, devices):
        s = (me + step) % devices
        remote(
            meta.at[pl.ds(0, local)], got_meta.at[s], meta_s.at[0], meta_r.at[s], {"dev": s}
        ).wait_recv()
        routing(s, got_meta[s])

    def arrive(s):
        block(s, 2, x_to).wait_recv()

    def from_line(zz, way, where, more):
        s = zz * COLS + x
        arrive(s)

        @pl.when(more)
        def _():
            block(s, way, where).start()

        block(s, 2, x_to).start()
        block(s, 3, core_to).start()
        dispatch(s, part, tok[part, s])

    def from_across(zz):
        s = zz * COLS + (1 - x)
        arrive(s)
        block(s, 3, core_to).start()
        dispatch(s, part, tok[part, s])

    def from_core(s):
        remote(tok.at[other, s], tok.at[other, s], ag_s.at[s, 3], core_r.at[s], core_to).wait_recv()
        dispatch(s, other, tok[other, s])

    def both(d, act):
        @pl.when(z - d >= 0)
        def _():
            act(z - d, True)

        @pl.when(z + d < lines)
        def _():
            act(z + d, False)

    for d in range(1, lines):
        both(d, lambda zz, low: from_line(
            zz, 0 if low else 1, up_to if low else down_to, not_top if low else not_bottom
        ))
        if d == 1:
            from_across(z)
        else:
            both(d - 1, lambda zz, low: from_core(zz * COLS + x))
    both(lines - 1, lambda zz, low: from_core(zz * COLS + x))
    from_core(across)
    for d in range(1, lines):
        both(d, lambda zz, low: from_across(zz))
        if d > 1:
            both(d - 1, lambda zz, low: from_core(zz * COLS + (1 - x)))
    both(lines - 1, lambda zz, low: from_core(zz * COLS + (1 - x)))

    @pl.when(not_top)
    def _():
        block(me, 0, up_to, mine).wait_send()

    @pl.when(not_bottom)
    def _():
        block(me, 1, down_to, mine).wait_send()

    block(me, 2, x_to, mine).wait_send()
    for d in range(1, lines):

        def sent(zz, low):
            s = zz * COLS + x

            @pl.when(not_top if low else not_bottom)
            def _():
                block(s, 0 if low else 1, up_to).wait_send()

            block(s, 2, x_to).wait_send()
            block(s, 3, core_to).wait_send()
            block(zz * COLS + (1 - x), 3, core_to).wait_send()

        both(d, sent)
    block(across, 3, core_to).wait_send()

    def hid_copy(h):
        return remote(hid_own.at[h], hid_other.at[h], hid_s.at[h], hid_r.at[h], core_to)

    def across_rows(left, right):
        return lax.dot_general(
            left, right, (((1,), (1,)), ((), ())), preferred_element_type=jnp.float32
        )

    def raise_expert(e):
        low, high = disp[0, e], disp[1, e]
        for b in range(2):
            h = 2 * e + b
            weight_copies(h)[0].wait()

            def product(g):
                return across_rows(low, gu[h, g, :, :half]) + across_rows(high, gu[h, g, :, half:])

            gate = product(0)
            hid_own[h] = (gate * jax.nn.sigmoid(gate) * product(1)).astype(jnp.bfloat16)
            hid_copy(h).start()

    def lower_expert(e):
        total = None
        for b in range(2):
            h = 2 * e + b
            weight_copies(h)[1].wait()
            hid_copy(h).wait_recv()
            first = dn[h, pl.ds(pl.multiple_of(part * hidden, SLOT), hidden), :]
            second = dn[h, pl.ds(pl.multiple_of(other * hidden, SLOT), hidden), :]
            piece = jnp.dot(hid_own[h], first, preferred_element_type=jnp.float32) + jnp.dot(
                hid_other[h], second, preferred_element_type=jnp.float32
            )
            piece = piece.astype(jnp.bfloat16).astype(jnp.float32)
            total = piece if total is None else total + piece
        gain = slot_gate[e][:, :1]
        disp[0, e] = (total * gain).astype(jnp.bfloat16)

    raise_expert(0)

    def step_expert(e, carry):
        raise_expert(e)
        lower_expert(e - 1)
        return carry

    lax.fori_loop(1, local, step_expert, 0)
    lower_expert(local - 1)

    def combine(s):
        rows = disp[0, :, pl.ds(pl.multiple_of(s * SLOT, SLOT), SLOT), :].reshape(slots, half)
        return lax.dot_general(
            pick[s], rows, (((0,), (0,)), ((), ())), preferred_element_type=jnp.float32
        )

    def x_copy(zz):
        return remote(
            tok.at[0, zz * COLS + (1 - x)], got_x.at[zz], x_s.at[zz], x_r.at[zz], x_to
        )

    def line_copy(zz, low):
        if low:
            return remote(tok.at[1, zz], got_down.at[zz], down_s.at[zz], down_r.at[zz], down_to)
        return remote(tok.at[1, zz], got_up.at[zz], up_s.at[zz], up_r.at[zz], up_to)

    def give_across(zz, low):
        s = zz * COLS + (1 - x)
        tok[0, s] = combine(s).astype(jnp.bfloat16)
        x_copy(zz).start()

    def add_line(zz, low):
        line_copy(zz, low).wait_recv()
        acc[...] += (got_down if low else got_up)[zz].astype(jnp.float32)

    def gather_here(zz):
        acc[...] = combine(zz * COLS + x)
        x_copy(zz).wait_recv()
        acc[...] += got_x[zz].astype(jnp.float32)

    def pass_on(zz, low):
        gather_here(zz)

        @pl.when(not_top if low else not_bottom)
        def _():
            add_line(zz, low)

        tok[1, zz] = acc[...].astype(jnp.bfloat16)
        line_copy(zz, low).start()

    for d in range(lines - 1, 0, -1):
        both(d, give_across)
    give_across(z, False)
    for d in range(lines - 1, 0, -1):
        both(d, pass_on)
    gather_here(z)

    @pl.when(not_bottom)
    def _():
        add_line(z, False)

    @pl.when(not_top)
    def _():
        add_line(z, True)

    own = pl.ds(pl.multiple_of(part * half, LANES), half)
    out[...] = (state[:, own] + (1.0 + modulation[3:4, own]) * acc[...]).astype(out.dtype)

    for d in range(1, lines):

        def drained(zz, low):
            line_copy(zz, low).wait_send()
            x_copy(zz).wait_send()

        both(d, drained)
    x_copy(z).wait_send()
    for step in range(1, devices):
        meta_copy(step).wait_send()

    def hid_drain(h, carry):
        hid_copy(h).wait_send()
        return carry

    lax.fori_loop(0, halves, hid_drain, 0)


def front_kernel(
    devices, start_weights,
    sources, held, own_sem,
    normed, state, meta,
    near, wide, mixed, mine_out, their_out,
    near_s, near_r, far_s, far_r, ag_s, ag_r, y_r, sum_s, sum_r,
):
    packed_hbm, weight_hbm = sources[1], sources[2]
    tokens, packed, weight, modulation, router, ids = held

    def own_copy(i):
        return pltpu.make_async_copy(sources[i], held[i], own_sem.at[i])

    for i in (1, 2, 0, 3, 4, 5):
        own_copy(i).start()
    me = lax.axis_index("dev")
    part = lax.axis_index("sub")
    group = lax.axis_index("groups")
    z = me // COLS
    x = me % COLS
    across = z * COLS + (1 - x)
    lines = devices // COLS
    count, width = tokens.shape
    shard = weight.shape[0]
    extra = shard * 3 // 8 // SLOT * SLOT
    main = shard - extra
    not_top = z < lines - 1
    not_bottom = z > 0
    up_to = {"dev": jnp.minimum(me + COLS, devices - 1)}
    down_to = {"dev": jnp.maximum(me - COLS, 0)}
    x_to = {"dev": across}
    y_to = {"groups": 1 - group}
    core_to = {"sub": 1 - part}

    barrier = pltpu.get_barrier_semaphore()
    for step in range(1, devices):
        pl.semaphore_signal(
            barrier, inc=1, device_id={"dev": (me + step) % devices}, device_id_type=MESH
        )
    pl.semaphore_signal(barrier, inc=1, device_id=core_to, device_id_type=MESH)
    pl.semaphore_signal(barrier, inc=1, device_id=y_to, device_id_type=MESH)
    pl.semaphore_wait(barrier, devices + 1)

    def remote(src, dst, send, recv, where):
        return pltpu.make_async_remote_copy(
            src_ref=src, dst_ref=dst, send_sem=send, recv_sem=recv,
            device_id=where, device_id_type=MESH,
        )

    def near_copy(i):
        return remote(packed_hbm.at[1 + i], near.at[x, i], near_s.at[i], near_r.at[i], x_to)

    def far_copy(i, where):
        return remote(near.at[1 - x, i], near.at[x, i], far_s.at[i], far_r.at[i], where)

    def piece(s, way, where, src=None):
        start, size = (main, extra) if way == 3 else (extra, main)
        dst = wide.at[s, pl.ds(pl.multiple_of(group * start, SLOT), size)]
        recv = y_r.at[s] if way == 3 else ag_r.at[s]
        return remote(dst if src is None else src, dst, ag_s.at[s, way], recv, where)

    far_up = (x == 0) & not_top
    far_down = (x == 1) & not_bottom
    have_far = ((x == 0) & not_bottom) | ((x == 1) & not_top)
    mine = weight_hbm.at[pl.ds(pl.multiple_of(group * extra, SLOT), main)]

    for i in range(2):
        near_copy(i).start()

    @pl.when(not_top)
    def _():
        piece(me, 0, up_to, mine).start()

    @pl.when(not_bottom)
    def _():
        piece(me, 1, down_to, mine).start()

    piece(me, 2, x_to, mine).start()
    start_weights()

    @pl.when(jnp.logical_not(have_far))
    def _():
        near[x] = jnp.zeros_like(near[x])

    for i in range(2):
        near_copy(i).wait_recv()

        @pl.when(far_up)
        def _():
            far_copy(i, up_to).start()

        @pl.when(far_down)
        def _():
            far_copy(i, down_to).start()

    def both(d, act):
        @pl.when(z - d >= 0)
        def _():
            act(z - d, True)

        @pl.when(z + d < lines)
        def _():
            act(z + d, False)

    def project(s, block):
        mine_out[s] = lax.dot_general(
            mixed[...], block, (((1,), (1,)), ((), ())), preferred_element_type=jnp.float32
        )
        sum_copy(s).start()

    def sum_copy(s):
        return remote(mine_out.at[s], their_out.at[s], sum_s.at[s], sum_r.at[s], core_to)

    def take_line(zz, low):
        s = zz * COLS + x
        piece(s, 2, x_to).wait_recv()

        @pl.when(not_top if low else not_bottom)
        def _():
            piece(s, 0 if low else 1, up_to if low else down_to).start()

        piece(s, 2, x_to).start()
        piece(s, 3, y_to).start()

    def take_across(zz, low):
        s = zz * COLS + (1 - x)
        piece(s, 2, x_to).wait_recv()
        piece(s, 3, y_to).start()

    def take_y(s):
        dst = wide.at[s, pl.ds(pl.multiple_of((1 - group) * main, SLOT), extra)]
        remote(dst, dst, ag_s.at[s, 3], y_r.at[s], y_to).wait_recv()
        project(s, wide[s])

    def line_y(zz, low):
        take_y(zz * COLS + x)

    def across_y(zz, low):
        take_y(zz * COLS + (1 - x))

    both(1, take_line)
    take_across(z, False)
    for d in range(2, min(3, lines)):
        both(d, take_line)
    for i in range(6):
        own_copy(i).wait()

    @pl.when(have_far)
    def _():
        for i in range(2):
            far_copy(i, x_to).wait_recv()

    row = lax.broadcasted_iota(jnp.int32, (count, count), 0)
    col = lax.broadcasted_iota(jnp.int32, (count, count), 1)
    see_before = (col >= row) & (me > 0)
    see_after = (col <= row) & (me < devices - 1)
    for h in range(mixed.shape[1] // HEAD):
        lanes = slice(h * HEAD, (h + 1) * HEAD)
        query = packed[0, :, lanes]

        def score(keys):
            return lax.dot_general(
                query, keys, (((1,), (1,)), ((), ())), preferred_element_type=jnp.float32
            ) / math.sqrt(HEAD)

        scores = jnp.concatenate(
            [
                jnp.where(see_before, score(near[0, 0, :, lanes]), NEG),
                score(packed[1, :, lanes]),
                jnp.where(see_after, score(near[1, 0, :, lanes]), NEG),
            ],
            axis=1,
        )
        top = jnp.max(scores, -1, keepdims=True)
        share = jnp.exp(scores - top)
        share = (share / jnp.sum(share, -1, keepdims=True)).astype(jnp.bfloat16)
        values = jnp.concatenate(
            [near[0, 1, :, lanes], packed[2, :, lanes], near[1, 1, :, lanes]], axis=0
        )
        mixed[:, lanes] = jnp.dot(
            share, values, preferred_element_type=jnp.float32
        ).astype(jnp.bfloat16)

    project(me, weight[...])
    for d in range(3, lines):
        both(d, take_line)
    for d in range(1, lines):
        both(d, line_y)
        both(d, take_across)
        if d == 1:
            take_y(across)
    for d in range(1, lines):
        both(d, across_y)

    square = jnp.zeros((count, 1), jnp.float32)
    for s in range(devices):
        sum_copy(s).wait_recv()
        lanes = slice(s * shard, (s + 1) * shard)
        value = tokens[:, lanes].astype(jnp.float32) + (1.0 + modulation[0:1, lanes]) * (
            mine_out[s] + their_out[s]
        )
        state[:, lanes] = value
        square = square + jnp.sum(value * value, -1, keepdims=True)
    scale = lax.rsqrt(square / width + EPS)
    for s in range(devices):
        lanes = slice(s * shard, (s + 1) * shard)
        normed[:, lanes] = (
            state[:, lanes] * scale * (1.0 + modulation[2:3, lanes]) + modulation[1:2, lanes]
        ).astype(jnp.bfloat16)
    logits = lax.dot_general(
        router[...], normed[...], (((1,), (1,)), ((), ())), preferred_element_type=jnp.float32
    )
    name = lax.broadcasted_iota(jnp.int32, logits.shape, 0)
    named = name == ids[0:1]
    for k in range(1, ids.shape[0]):
        named = named | (name == ids[k:k + 1])
    lifted = jnp.where(named, jax.nn.sigmoid(logits), 0.0)
    meta[...] = lifted / jnp.sum(lifted, 0, keepdims=True)

    for i in range(2):
        near_copy(i).wait_send()

        @pl.when(far_up | far_down)
        def _():
            far_copy(i, x_to).wait_send()

    @pl.when(not_top)
    def _():
        piece(me, 0, up_to, mine).wait_send()

    @pl.when(not_bottom)
    def _():
        piece(me, 1, down_to, mine).wait_send()

    piece(me, 2, x_to, mine).wait_send()
    piece(across, 3, y_to).wait_send()
    for d in range(1, lines):

        def sent(zz, low):
            s = zz * COLS + x

            @pl.when(not_top if low else not_bottom)
            def _():
                piece(s, 0 if low else 1, up_to).wait_send()

            piece(s, 2, x_to).wait_send()
            piece(s, 3, y_to).wait_send()
            piece(zz * COLS + (1 - x), 3, y_to).wait_send()

        both(d, sent)
    for s in range(devices):
        sum_copy(s).wait_send()


def block_kernel(devices, *refs):
    sources, gate_up, down, out = refs[:6], refs[6], refs[7], refs[8]
    held, normed, state, meta = refs[9:15], refs[15], refs[16], refs[17]
    front_buffers, expert_buffers = refs[18:23], refs[23:36]
    own_sem, gu_sem, dn_sem = refs[36:39]
    front_sems, expert_sems = refs[39:48], refs[48:]
    gu, dn = expert_buffers[2:4]
    halves = gate_up.shape[0]

    def weight_copies(h):
        return (
            pltpu.make_async_copy(gate_up.at[h], gu.at[h], gu_sem.at[h]),
            pltpu.make_async_copy(down.at[h], dn.at[h], dn_sem.at[h]),
        )

    def start_weights():
        def one(h, carry):
            for copy in weight_copies(h):
                copy.start()
            return carry

        lax.fori_loop(0, halves, one, 0)

    front_kernel(
        devices, start_weights, sources, held, own_sem, normed, state, meta,
        *front_buffers, *front_sems,
    )
    expert_kernel(
        devices, weight_copies, normed, meta, state, held[3], gate_up, down, out,
        *expert_buffers, *expert_sems,
    )


def block_call(
    tokens, query_key_value, out_weight, modulation, router_weight, expert_ids,
    gate_up_weight, down_weight,
):
    devices = lax.axis_size("dev")
    count, width = tokens.shape
    half = down_weight.shape[2]
    halves = gate_up_weight.shape[0]
    local = halves // 2
    gate_up_weight = gate_up_weight.swapaxes(2, 3)
    hidden = gate_up_weight.shape[2]
    lines = devices // COLS
    rows = devices * SLOT
    shard = out_weight.shape[0]
    own = (
        tokens, query_key_value.transpose(1, 0, 2), out_weight, modulation,
        router_weight.T, expert_ids.T,
    )
    hbm = pl.BlockSpec(memory_space=pl.ANY)
    dma = pltpu.SemaphoreType.DMA
    return pl.pallas_call(
        functools.partial(block_kernel, devices),
        out_shape=jax.ShapeDtypeStruct((count, half), jnp.bfloat16),
        in_specs=[hbm] * 8,
        out_specs=pl.BlockSpec(memory_space=pltpu.VMEM),
        scratch_shapes=[
            *[pltpu.VMEM(array.shape, array.dtype) for array in own],
            pltpu.VMEM((count, width), jnp.bfloat16),
            pltpu.VMEM((count, width), jnp.float32),
            pltpu.VMEM((router_weight.shape[1], count), jnp.float32),
            pltpu.VMEM((2, 2, count, half), jnp.bfloat16),
            pltpu.VMEM((devices, shard, half), jnp.bfloat16),
            pltpu.VMEM((count, half), jnp.bfloat16),
            pltpu.VMEM((devices, count, shard), jnp.float32),
            pltpu.VMEM((devices, count, shard), jnp.float32),
            pltpu.VMEM((2, devices, count, half), jnp.bfloat16),
            pltpu.VMEM((2, local, rows, half), jnp.bfloat16),
            pltpu.VMEM(gate_up_weight.shape, jnp.bfloat16),
            pltpu.VMEM(down_weight.shape, jnp.bfloat16),
            pltpu.VMEM((halves, rows, hidden), jnp.bfloat16),
            pltpu.VMEM((halves, rows, hidden), jnp.bfloat16),
            pltpu.VMEM((devices, local, count), jnp.float32),
            pltpu.VMEM((devices, local * SLOT, count), jnp.bfloat16),
            pltpu.VMEM((local, rows, LANES), jnp.float32),
            pltpu.VMEM((lines, count, half), jnp.bfloat16),
            pltpu.VMEM((lines, count, half), jnp.bfloat16),
            pltpu.VMEM((lines, count, half), jnp.bfloat16),
            pltpu.VMEM((count, half), jnp.float32),
            dma((6,)), dma((halves,)), dma((halves,)),
            dma((2,)), dma((2,)), dma((2,)), dma((2,)),
            dma((devices, 4)), dma((devices,)), dma((devices,)),
            dma((devices,)), dma((devices,)),
            dma((devices,)), dma((devices,)), dma((devices, 4)), dma((devices,)), dma((devices,)),
            dma((halves,)), dma((halves,)),
            dma((lines,)), dma((lines,)), dma((lines,)), dma((lines,)), dma((lines,)), dma((lines,)),
        ],
        compiler_params=pltpu.CompilerParams(
            collective_id=1, has_side_effects=True, vmem_limit_bytes=VMEM_BYTES
        ),
    )(*own, gate_up_weight, down_weight)


def body(
    tokens,
    query_key_value,
    out_weight,
    modulation,
    router_weight,
    expert_ids,
    gate_up_weight,
    down_weight,
):
    count = tokens.shape[0]
    width = tokens.shape[1]
    parts = lax.axis_size("sub")
    part = lax.axis_index("sub")
    position = lax.axis_index("dev")
    devices = lax.axis_size("dev")
    total = count * devices
    local_width = query_key_value.shape[2]
    weight_bytes = 2 * (gate_up_weight.size + down_weight.size)
    token_bytes = 12 * devices * count * width
    fits = weight_bytes + token_bytes < VMEM_BYTES and CAP <= SLOT
    paired = parts == 2 and lax.axis_size("groups") == 2 and devices % COLS == 0
    tiled = out_weight.shape[0] % (2 * LANES) == 0 and count == LANES
    if fits and paired and tiled:
        return block_call(
            tokens, query_key_value, out_weight, modulation, router_weight, expert_ids,
            gate_up_weight, down_weight,
        )
    heads_here = local_width // HEAD
    query = query_key_value[:, 0].reshape(count, heads_here, HEAD)
    pair = query_key_value[:, 1:]
    near = extended(pair, (("dev", 0),), count)
    keys = near[:, 0].reshape(3 * count, heads_here, HEAD)
    values = near[:, 1].reshape(3 * count, heads_here, HEAD)
    mixed = window_attention(query, keys, values, position, total).reshape(count, local_width)
    partial_proj = lax.dot_general(
        mixed,
        lax.all_gather(out_weight, "dev", axis=0, tiled=True),
        (((1,), (1,)), ((), ())),
        preferred_element_type=jnp.float32,
    )
    proj = lax.psum(partial_proj, "sub")
    state = tokens.astype(jnp.float32) + (1.0 + modulation[0]) * proj
    normed = normalize(state, modulation)
    gates = route(normed, router_weight, expert_ids)
    experts = router_weight.shape[1]
    topk = expert_ids.shape[1]
    flat = expert_ids.reshape(-1)
    picks = flat.shape[0]
    onehot = (flat[:, None] == jnp.arange(experts, dtype=jnp.int32)[None, :]).astype(jnp.int32)
    rank = jnp.sum((jnp.cumsum(onehot, 0) - 1) * onehot, 1)
    target = flat * CAP + rank
    hit = target[None, :] == jnp.arange(experts * CAP, dtype=jnp.int32)[:, None]
    filled = jnp.any(hit, 1)
    anchor = jnp.sum(jnp.where(hit, jnp.arange(picks, dtype=jnp.int32)[None, :], 0), 1) // topk
    slice_width = width // parts
    sent = lax.dynamic_slice_in_dim(normed, part * slice_width, slice_width, 1)
    sent_width = sent.shape[1]
    rows_out = jnp.where(filled[:, None], sent[anchor], jnp.zeros((), jnp.bfloat16))
    halves_here = gate_up_weight.shape[0]
    doubled = jnp.broadcast_to(
        rows_out.reshape(experts, 1, CAP, sent_width), (experts, 2, CAP, sent_width)
    )
    outgoing = doubled.reshape(devices, halves_here, CAP, sent_width)
    up_form = "sxcd,xgdf->sxcgf"
    down_form = "sxcf,xfd->sxcd"
    incoming = lax.all_to_all(outgoing, "dev", split_axis=0, concat_axis=0, tiled=True)
    both = jnp.einsum(
        up_form,
        lax.all_gather(incoming, "sub", axis=3, tiled=True),
        gate_up_weight,
        preferred_element_type=jnp.float32,
    )
    hidden = (jax.nn.silu(both[..., 0, :]) * both[..., 1, :]).astype(jnp.bfloat16)
    gathered = lax.all_gather(hidden, "sub", axis=hidden.ndim - 1, tiled=True)
    result = jnp.einsum(down_form, gathered, down_weight, preferred_element_type=jnp.float32)
    returned = lax.all_to_all(
        result.astype(jnp.bfloat16), "dev", split_axis=0, concat_axis=0, tiled=True
    )
    own_width = returned.shape[-1]
    arranged = returned.reshape(experts, 2, CAP, own_width)
    answers = arranged[flat, :, rank, :].reshape(count, topk, 2, own_width).astype(jnp.float32)
    combined = answers[:, :, 0] + answers[:, :, 1]
    routed = jnp.einsum("tk,tkd->td", gates, combined)
    own = lax.dynamic_slice_in_dim(state, part * slice_width, slice_width, 1)
    lift = lax.dynamic_slice_in_dim(modulation[3], part * slice_width, slice_width, 0)
    return (own + (1.0 + lift) * routed).astype(jnp.bfloat16)


def solution(mesh):
    return jax.shard_map(
        body,
        mesh=mesh,
        in_specs=(
            P(("groups", "dev"), None),
            P(("groups", "dev"), None, "sub"),
            P("dev", "sub"),
            P("groups", None),
            P(),
            P(("groups", "dev"), None),
            P("dev", None, None, "sub"),
            P("dev", None, "sub"),
        ),
        out_specs=P(("groups", "dev"), "sub"),
        check_vma=False,
    )
```

```python
import functools
import math

import jax
import jax.numpy as jnp
from jax import lax
from jax.experimental import pallas as pl
from jax.experimental.pallas import tpu as pltpu
from jax.sharding import PartitionSpec as P

HEAD = 128
CAP = 12


EPS = 1e-06
NEG = -1e30


def extended(cells, sides, width):
    for axis, dim in sides:
        count = lax.axis_size(axis)
        ends = count - 1
        head = lax.slice_in_dim(cells, 0, width, axis=dim)
        tail = lax.slice_in_dim(cells, cells.shape[dim] - width, cells.shape[dim], axis=dim)
        cells = jnp.concatenate(
            [
                lax.ppermute(tail, axis, [(i, (i + 1) % count) for i in range(ends)]),
                cells,
                lax.ppermute(head, axis, [((i + 1) % count, i) for i in range(ends)]),
            ],
            axis=dim,
        )
    return cells


def window_attention(query, keys, values, index, total):
    count = query.shape[0]
    rows = jnp.arange(count, dtype=jnp.int32)[:, None]
    cols = jnp.arange(3 * count, dtype=jnp.int32)[None, :] - count
    place = index * count + cols
    allowed = (jnp.abs(cols - rows) <= count) & (place >= 0) & (place < total)
    scores = jnp.einsum(
        "qhd,khd->hqk", query, keys, preferred_element_type=jnp.float32
    ) / math.sqrt(query.shape[2])
    scores = jnp.where(allowed[None], scores, NEG)
    top = jnp.max(scores, -1, keepdims=True)
    weight = jnp.exp(scores - top)
    weight = (weight / jnp.sum(weight, -1, keepdims=True)).astype(jnp.bfloat16)
    mixed = jnp.einsum("hqk,khd->qhd", weight, values, preferred_element_type=jnp.float32)
    return mixed.astype(jnp.bfloat16)


def normalize(state, modulation):
    scale = lax.rsqrt(jnp.mean(state * state, -1, keepdims=True) + EPS)
    return (state * scale * (1.0 + modulation[2]) + modulation[1]).astype(jnp.bfloat16)


def route(normed, router_weight, expert_ids):
    logits = jnp.dot(normed, router_weight, preferred_element_type=jnp.float32)
    experts = router_weight.shape[1]
    match = expert_ids[:, :, None] == jnp.arange(experts, dtype=jnp.int32)[None, None, :]
    picked = jnp.sum(jnp.where(match, logits[:, None, :], 0.0), -1)
    lifted = jax.nn.sigmoid(picked)
    return lifted / jnp.sum(lifted, -1, keepdims=True)


LANES = 128
SLOT = 16
COLS = 2
PIECES = 2
VMEM_BYTES = 66 * 1000 * 1000
MESH = pl.DeviceIdType.MESH


def expert_kernel(
    devices, weight_copies,
    normed, meta, state, modulation, gate_up, down,
    out,
    tok, disp, gu, dn, hid_own, hid_other, got_meta, pick, slot_gate, got_x, got_up, got_down, acc,
    meta_s, meta_r, ag_s, ag_r, core_r, hid_s, hid_r,
    x_s, x_r, up_s, up_r, down_s, down_r,
):
    me = lax.axis_index("dev")
    part = lax.axis_index("sub")
    other = 1 - part
    z = me // COLS
    x = me % COLS
    across = z * COLS + (1 - x)
    lines = devices // COLS
    count, width = normed.shape
    half = width // 2
    halves = gate_up.shape[0]
    local = halves // 2
    hidden = gate_up.shape[2]
    slots = local * SLOT

    def remote(src, dst, send, recv, where):
        return pltpu.make_async_remote_copy(
            src_ref=src, dst_ref=dst, send_sem=send, recv_sem=recv,
            device_id=where, device_id_type=MESH,
        )

    def block(s, way, where, src=None):
        dst = tok.at[part, s]
        recv = core_r.at[s] if way == 3 else ag_r.at[s]
        return remote(dst if src is None else src, dst, ag_s.at[s, way], recv, where)

    up_to = {"dev": jnp.minimum(me + COLS, devices - 1)}
    down_to = {"dev": jnp.maximum(me - COLS, 0)}
    x_to = {"dev": across}
    core_to = {"sub": other}
    not_top = z < lines - 1
    not_bottom = z > 0
    mine = normed.at[:, pl.ds(pl.multiple_of(part * half, LANES), half)]

    def meta_copy(step):
        target = (me + step) % devices
        return remote(
            meta.at[pl.ds(pl.multiple_of(target * local, local), local)], got_meta.at[me],
            meta_s.at[step - 1], meta_r.at[me], {"dev": target},
        )

    for step in range(1, devices):
        meta_copy(step).start()

    @pl.when(not_top)
    def _():
        block(me, 0, up_to, mine).start()

    @pl.when(not_bottom)
    def _():
        block(me, 1, down_to, mine).start()

    block(me, 2, x_to, mine).start()

    before = (
        lax.broadcasted_iota(jnp.int32, (count, count), 0)
        < lax.broadcasted_iota(jnp.int32, (count, count), 1)
    ).astype(jnp.float32).astype(jnp.bfloat16)
    place = lax.broadcasted_iota(jnp.int32, (local, SLOT, count), 1).astype(jnp.float32)

    def routing(s, gate):
        chosen = jnp.where(gate > 0.0, 1.0, 0.0)
        rank = jnp.dot(chosen.astype(jnp.bfloat16), before, preferred_element_type=jnp.float32)
        rank = jnp.where(gate > 0.0, rank, -1.0)
        hit = jnp.broadcast_to(rank[:, None, :], place.shape) == place
        pick[s] = jnp.where(hit, 1.0, 0.0).reshape(slots, count).astype(jnp.bfloat16)
        value = jnp.where(hit, jnp.broadcast_to(gate[:, None, :], place.shape), 0.0)
        value = jnp.sum(value, -1, keepdims=True)
        slot_gate[:, pl.ds(pl.multiple_of(s * SLOT, SLOT), SLOT), :] = jnp.broadcast_to(
            value, (local, SLOT, LANES)
        )

    def dispatch(s, h, rows):
        moved = jnp.dot(pick[s], rows, preferred_element_type=jnp.float32)
        disp[h, :, pl.ds(pl.multiple_of(s * SLOT, SLOT), SLOT), :] = moved.astype(
            jnp.bfloat16
        ).reshape(local, SLOT, half)

    routing(me, meta[pl.ds(pl.multiple_of(me * local, local), local)])
    dispatch(me, 0, normed[:, :half])
    dispatch(me, 1, normed[:, half:])
    for step in range(1, devices):
        s = (me + step) % devices
        remote(
            meta.at[pl.ds(0, local)], got_meta.at[s], meta_s.at[0], meta_r.at[s], {"dev": s}
        ).wait_recv()
        routing(s, got_meta[s])

    def arrive(s):
        block(s, 2, x_to).wait_recv()

    def from_line(zz, way, where, more):
        s = zz * COLS + x
        arrive(s)

        @pl.when(more)
        def _():
            block(s, way, where).start()

        block(s, 2, x_to).start()
        block(s, 3, core_to).start()
        dispatch(s, part, tok[part, s])

    def from_across(zz):
        s = zz * COLS + (1 - x)
        arrive(s)
        block(s, 3, core_to).start()
        dispatch(s, part, tok[part, s])

    def from_core(s):
        remote(tok.at[other, s], tok.at[other, s], ag_s.at[s, 3], core_r.at[s], core_to).wait_recv()
        dispatch(s, other, tok[other, s])

    def both(d, act):
        @pl.when(z - d >= 0)
        def _():
            act(z - d, True)

        @pl.when(z + d < lines)
        def _():
            act(z + d, False)

    for d in range(1, lines):
        both(d, lambda zz, low: from_line(
            zz, 0 if low else 1, up_to if low else down_to, not_top if low else not_bottom
        ))
        if d == 1:
            from_across(z)
        else:
            both(d - 1, lambda zz, low: from_core(zz * COLS + x))
    both(lines - 1, lambda zz, low: from_core(zz * COLS + x))
    from_core(across)
    for d in range(1, lines):
        both(d, lambda zz, low: from_across(zz))
        if d > 1:
            both(d - 1, lambda zz, low: from_core(zz * COLS + (1 - x)))
    both(lines - 1, lambda zz, low: from_core(zz * COLS + (1 - x)))

    @pl.when(not_top)
    def _():
        block(me, 0, up_to, mine).wait_send()

    @pl.when(not_bottom)
    def _():
        block(me, 1, down_to, mine).wait_send()

    block(me, 2, x_to, mine).wait_send()
    for d in range(1, lines):

        def sent(zz, low):
            s = zz * COLS + x

            @pl.when(not_top if low else not_bottom)
            def _():
                block(s, 0 if low else 1, up_to).wait_send()

            block(s, 2, x_to).wait_send()
            block(s, 3, core_to).wait_send()
            block(zz * COLS + (1 - x), 3, core_to).wait_send()

        both(d, sent)
    block(across, 3, core_to).wait_send()

    def hid_copy(h):
        return remote(hid_own.at[h], hid_other.at[h], hid_s.at[h], hid_r.at[h], core_to)

    def across_rows(left, right):
        return lax.dot_general(
            left, right, (((1,), (1,)), ((), ())), preferred_element_type=jnp.float32
        )

    def raise_expert(e):
        low, high = disp[0, e], disp[1, e]
        for b in range(2):
            h = 2 * e + b
            weight_copies(h)[0].wait()

            def product(g):
                return across_rows(low, gu[h, g, :, :half]) + across_rows(high, gu[h, g, :, half:])

            gate = product(0)
            hid_own[h] = (gate * jax.nn.sigmoid(gate) * product(1)).astype(jnp.bfloat16)
            hid_copy(h).start()

    cut = half // PIECES

    def columns(c):
        return slice(c * cut, (c + 1) * cut)

    def lower_expert(e, c):
        total = None
        for b in range(2):
            h = 2 * e + b
            if c == 0:
                weight_copies(h)[1].wait()
                hid_copy(h).wait_recv()
            first = dn[h, pl.ds(pl.multiple_of(part * hidden, SLOT), hidden), columns(c)]
            second = dn[h, pl.ds(pl.multiple_of(other * hidden, SLOT), hidden), columns(c)]
            piece = jnp.dot(hid_own[h], first, preferred_element_type=jnp.float32) + jnp.dot(
                hid_other[h], second, preferred_element_type=jnp.float32
            )
            piece = piece.astype(jnp.bfloat16).astype(jnp.float32)
            total = piece if total is None else total + piece
        gain = slot_gate[e][:, :1]
        disp[0, e, :, columns(c)] = (total * gain).astype(jnp.bfloat16)

    def each_expert(act):
        def step(e, carry):
            act(e)
            return carry

        lax.fori_loop(0, local, step, 0)

    def combine(s, c):
        rows = disp[0, :, pl.ds(pl.multiple_of(s * SLOT, SLOT), SLOT), columns(c)]
        return lax.dot_general(
            pick[s], rows.reshape(slots, cut), (((0,), (0,)), ((), ())),
            preferred_element_type=jnp.float32,
        )

    def x_copy(zz, c):
        return remote(
            tok.at[0, zz * COLS + (1 - x), :, columns(c)], got_x.at[zz, :, columns(c)],
            x_s.at[zz, c], x_r.at[zz, c], x_to,
        )

    def line_copy(zz, low, c):
        src = tok.at[1, zz, :, columns(c)]
        if low:
            return remote(
                src, got_down.at[zz, :, columns(c)], down_s.at[zz, c], down_r.at[zz, c], down_to
            )
        return remote(src, got_up.at[zz, :, columns(c)], up_s.at[zz, c], up_r.at[zz, c], up_to)

    def give_across(zz, c):
        s = zz * COLS + (1 - x)
        tok[0, s, :, columns(c)] = combine(s, c).astype(jnp.bfloat16)
        x_copy(zz, c).start()

    def add_line(zz, low, c):
        line_copy(zz, low, c).wait_recv()
        came = (got_down if low else got_up)[zz, :, columns(c)]
        acc[:, columns(c)] += came.astype(jnp.float32)

    def gather_here(zz, c):
        acc[:, columns(c)] = combine(zz * COLS + x, c)
        x_copy(zz, c).wait_recv()
        acc[:, columns(c)] += got_x[zz, :, columns(c)].astype(jnp.float32)

    def pass_on(zz, low, c):
        gather_here(zz, c)

        @pl.when(not_top if low else not_bottom)
        def _():
            add_line(zz, low, c)

        tok[1, zz, :, columns(c)] = acc[:, columns(c)].astype(jnp.bfloat16)
        line_copy(zz, low, c).start()

    each_expert(raise_expert)
    for c in range(PIECES):
        each_expert(lambda e: lower_expert(e, c))
        for d in range(lines - 1, 0, -1):
            both(d, lambda zz, low: give_across(zz, c))
        give_across(z, c)
    for c in range(PIECES):
        for d in range(lines - 1, 0, -1):
            both(d, lambda zz, low: pass_on(zz, low, c))
    for c in range(PIECES):
        gather_here(z, c)

        @pl.when(not_bottom)
        def _():
            add_line(z, False, c)

        @pl.when(not_top)
        def _():
            add_line(z, True, c)

        own = pl.ds(pl.multiple_of(part * half + c * cut, LANES), cut)
        out[:, columns(c)] = (
            state[:, own] + (1.0 + modulation[3:4, own]) * acc[:, columns(c)]
        ).astype(out.dtype)

    for c in range(PIECES):
        for d in range(1, lines):

            def drained(zz, low):
                line_copy(zz, low, c).wait_send()
                x_copy(zz, c).wait_send()

            both(d, drained)
        x_copy(z, c).wait_send()
    for step in range(1, devices):
        meta_copy(step).wait_send()

    def hid_drain(h, carry):
        hid_copy(h).wait_send()
        return carry

    lax.fori_loop(0, halves, hid_drain, 0)


def front_kernel(
    devices, start_weights,
    sources, held, own_sem,
    normed, state, meta,
    near, wide, mixed, mine_out, their_out,
    near_s, near_r, far_s, far_r, ag_s, ag_r, y_r, sum_s, sum_r,
):
    packed_hbm, weight_hbm = sources[1], sources[2]
    tokens, packed, weight, modulation, router, ids = held

    def own_copy(i):
        return pltpu.make_async_copy(sources[i], held[i], own_sem.at[i])

    for i in (1, 2, 0, 3, 4, 5):
        own_copy(i).start()
    me = lax.axis_index("dev")
    part = lax.axis_index("sub")
    group = lax.axis_index("groups")
    z = me // COLS
    x = me % COLS
    across = z * COLS + (1 - x)
    lines = devices // COLS
    count, width = tokens.shape
    shard = weight.shape[0]
    extra = shard * 3 // 8 // SLOT * SLOT
    main = shard - extra
    not_top = z < lines - 1
    not_bottom = z > 0
    up_to = {"dev": jnp.minimum(me + COLS, devices - 1)}
    down_to = {"dev": jnp.maximum(me - COLS, 0)}
    x_to = {"dev": across}
    y_to = {"groups": 1 - group}
    core_to = {"sub": 1 - part}

    barrier = pltpu.get_barrier_semaphore()
    for step in range(1, devices):
        pl.semaphore_signal(
            barrier, inc=1, device_id={"dev": (me + step) % devices}, device_id_type=MESH
        )
    pl.semaphore_signal(barrier, inc=1, device_id=core_to, device_id_type=MESH)
    pl.semaphore_signal(barrier, inc=1, device_id=y_to, device_id_type=MESH)
    pl.semaphore_wait(barrier, devices + 1)

    def remote(src, dst, send, recv, where):
        return pltpu.make_async_remote_copy(
            src_ref=src, dst_ref=dst, send_sem=send, recv_sem=recv,
            device_id=where, device_id_type=MESH,
        )

    def near_copy(i):
        return remote(packed_hbm.at[1 + i], near.at[x, i], near_s.at[i], near_r.at[i], x_to)

    def far_copy(i, where):
        return remote(near.at[1 - x, i], near.at[x, i], far_s.at[i], far_r.at[i], where)

    def piece(s, way, where, src=None):
        start, size = (main, extra) if way == 3 else (extra, main)
        dst = wide.at[s, pl.ds(pl.multiple_of(group * start, SLOT), size)]
        recv = y_r.at[s] if way == 3 else ag_r.at[s]
        return remote(dst if src is None else src, dst, ag_s.at[s, way], recv, where)

    far_up = (x == 0) & not_top
    far_down = (x == 1) & not_bottom
    have_far = ((x == 0) & not_bottom) | ((x == 1) & not_top)
    mine = weight_hbm.at[pl.ds(pl.multiple_of(group * extra, SLOT), main)]

    for i in range(2):
        near_copy(i).start()

    @pl.when(not_top)
    def _():
        piece(me, 0, up_to, mine).start()

    @pl.when(not_bottom)
    def _():
        piece(me, 1, down_to, mine).start()

    piece(me, 2, x_to, mine).start()
    start_weights()

    @pl.when(jnp.logical_not(have_far))
    def _():
        near[x] = jnp.zeros_like(near[x])

    for i in range(2):
        near_copy(i).wait_recv()

        @pl.when(far_up)
        def _():
            far_copy(i, up_to).start()

        @pl.when(far_down)
        def _():
            far_copy(i, down_to).start()

    def both(d, act):
        @pl.when(z - d >= 0)
        def _():
            act(z - d, True)

        @pl.when(z + d < lines)
        def _():
            act(z + d, False)

    def project(s, block):
        mine_out[s] = lax.dot_general(
            mixed[...], block, (((1,), (1,)), ((), ())), preferred_element_type=jnp.float32
        )
        sum_copy(s).start()

    def sum_copy(s):
        return remote(mine_out.at[s], their_out.at[s], sum_s.at[s], sum_r.at[s], core_to)

    def take_line(zz, low):
        s = zz * COLS + x
        piece(s, 2, x_to).wait_recv()

        @pl.when(not_top if low else not_bottom)
        def _():
            piece(s, 0 if low else 1, up_to if low else down_to).start()

        piece(s, 2, x_to).start()
        piece(s, 3, y_to).start()

    def take_across(zz, low):
        s = zz * COLS + (1 - x)
        piece(s, 2, x_to).wait_recv()
        piece(s, 3, y_to).start()

    def take_y(s):
        dst = wide.at[s, pl.ds(pl.multiple_of((1 - group) * main, SLOT), extra)]
        remote(dst, dst, ag_s.at[s, 3], y_r.at[s], y_to).wait_recv()
        project(s, wide[s])

    def line_y(zz, low):
        take_y(zz * COLS + x)

    def across_y(zz, low):
        take_y(zz * COLS + (1 - x))

    both(1, take_line)
    take_across(z, False)
    for d in range(2, min(3, lines)):
        both(d, take_line)
    for i in range(6):
        own_copy(i).wait()

    @pl.when(have_far)
    def _():
        for i in range(2):
            far_copy(i, x_to).wait_recv()

    row = lax.broadcasted_iota(jnp.int32, (count, count), 0)
    col = lax.broadcasted_iota(jnp.int32, (count, count), 1)
    see_before = (col >= row) & (me > 0)
    see_after = (col <= row) & (me < devices - 1)
    for h in range(mixed.shape[1] // HEAD):
        lanes = slice(h * HEAD, (h + 1) * HEAD)
        query = packed[0, :, lanes]

        def score(keys):
            return lax.dot_general(
                query, keys, (((1,), (1,)), ((), ())), preferred_element_type=jnp.float32
            ) / math.sqrt(HEAD)

        scores = jnp.concatenate(
            [
                jnp.where(see_before, score(near[0, 0, :, lanes]), NEG),
                score(packed[1, :, lanes]),
                jnp.where(see_after, score(near[1, 0, :, lanes]), NEG),
            ],
            axis=1,
        )
        top = jnp.max(scores, -1, keepdims=True)
        share = jnp.exp(scores - top)
        share = (share / jnp.sum(share, -1, keepdims=True)).astype(jnp.bfloat16)
        values = jnp.concatenate(
            [near[0, 1, :, lanes], packed[2, :, lanes], near[1, 1, :, lanes]], axis=0
        )
        mixed[:, lanes] = jnp.dot(
            share, values, preferred_element_type=jnp.float32
        ).astype(jnp.bfloat16)

    project(me, weight[...])
    for d in range(3, lines):
        both(d, take_line)
    for d in range(1, lines):
        both(d, line_y)
        both(d, take_across)
        if d == 1:
            take_y(across)
    for d in range(1, lines):
        both(d, across_y)

    square = jnp.zeros((count, 1), jnp.float32)
    for s in range(devices):
        sum_copy(s).wait_recv()
        lanes = slice(s * shard, (s + 1) * shard)
        value = tokens[:, lanes].astype(jnp.float32) + (1.0 + modulation[0:1, lanes]) * (
            mine_out[s] + their_out[s]
        )
        state[:, lanes] = value
        square = square + jnp.sum(value * value, -1, keepdims=True)
    scale = lax.rsqrt(square / width + EPS)
    for s in range(devices):
        lanes = slice(s * shard, (s + 1) * shard)
        normed[:, lanes] = (
            state[:, lanes] * scale * (1.0 + modulation[2:3, lanes]) + modulation[1:2, lanes]
        ).astype(jnp.bfloat16)
    logits = lax.dot_general(
        router[...], normed[...], (((1,), (1,)), ((), ())), preferred_element_type=jnp.float32
    )
    name = lax.broadcasted_iota(jnp.int32, logits.shape, 0)
    named = name == ids[0:1]
    for k in range(1, ids.shape[0]):
        named = named | (name == ids[k:k + 1])
    lifted = jnp.where(named, jax.nn.sigmoid(logits), 0.0)
    meta[...] = lifted / jnp.sum(lifted, 0, keepdims=True)

    for i in range(2):
        near_copy(i).wait_send()

        @pl.when(far_up | far_down)
        def _():
            far_copy(i, x_to).wait_send()

    @pl.when(not_top)
    def _():
        piece(me, 0, up_to, mine).wait_send()

    @pl.when(not_bottom)
    def _():
        piece(me, 1, down_to, mine).wait_send()

    piece(me, 2, x_to, mine).wait_send()
    piece(across, 3, y_to).wait_send()
    for d in range(1, lines):

        def sent(zz, low):
            s = zz * COLS + x

            @pl.when(not_top if low else not_bottom)
            def _():
                piece(s, 0 if low else 1, up_to).wait_send()

            piece(s, 2, x_to).wait_send()
            piece(s, 3, y_to).wait_send()
            piece(zz * COLS + (1 - x), 3, y_to).wait_send()

        both(d, sent)
    for s in range(devices):
        sum_copy(s).wait_send()


def block_kernel(devices, *refs):
    sources, gate_up, down, out = refs[:6], refs[6], refs[7], refs[8]
    held, normed, state, meta = refs[9:15], refs[15], refs[16], refs[17]
    front_buffers, expert_buffers = refs[18:23], refs[23:36]
    own_sem, gu_sem, dn_sem = refs[36:39]
    front_sems, expert_sems = refs[39:48], refs[48:]
    gu, dn = expert_buffers[2:4]
    halves = gate_up.shape[0]

    def weight_copies(h):
        return (
            pltpu.make_async_copy(gate_up.at[h], gu.at[h], gu_sem.at[h]),
            pltpu.make_async_copy(down.at[h], dn.at[h], dn_sem.at[h]),
        )

    def start_weights():
        def one(h, carry):
            for copy in weight_copies(h):
                copy.start()
            return carry

        lax.fori_loop(0, halves, one, 0)

    front_kernel(
        devices, start_weights, sources, held, own_sem, normed, state, meta,
        *front_buffers, *front_sems,
    )
    expert_kernel(
        devices, weight_copies, normed, meta, state, held[3], gate_up, down, out,
        *expert_buffers, *expert_sems,
    )


def block_call(
    tokens, query_key_value, out_weight, modulation, router_weight, expert_ids,
    gate_up_weight, down_weight,
):
    devices = lax.axis_size("dev")
    count, width = tokens.shape
    half = down_weight.shape[2]
    halves = gate_up_weight.shape[0]
    local = halves // 2
    gate_up_weight = gate_up_weight.swapaxes(2, 3)
    hidden = gate_up_weight.shape[2]
    lines = devices // COLS
    rows = devices * SLOT
    shard = out_weight.shape[0]
    own = (
        tokens, query_key_value.transpose(1, 0, 2), out_weight, modulation,
        router_weight.T, expert_ids.T,
    )
    hbm = pl.BlockSpec(memory_space=pl.ANY)
    dma = pltpu.SemaphoreType.DMA
    return pl.pallas_call(
        functools.partial(block_kernel, devices),
        out_shape=jax.ShapeDtypeStruct((count, half), jnp.bfloat16),
        in_specs=[hbm] * 8,
        out_specs=pl.BlockSpec(memory_space=pltpu.VMEM),
        scratch_shapes=[
            *[pltpu.VMEM(array.shape, array.dtype) for array in own],
            pltpu.VMEM((count, width), jnp.bfloat16),
            pltpu.VMEM((count, width), jnp.float32),
            pltpu.VMEM((router_weight.shape[1], count), jnp.float32),
            pltpu.VMEM((2, 2, count, half), jnp.bfloat16),
            pltpu.VMEM((devices, shard, half), jnp.bfloat16),
            pltpu.VMEM((count, half), jnp.bfloat16),
            pltpu.VMEM((devices, count, shard), jnp.float32),
            pltpu.VMEM((devices, count, shard), jnp.float32),
            pltpu.VMEM((2, devices, count, half), jnp.bfloat16),
            pltpu.VMEM((2, local, rows, half), jnp.bfloat16),
            pltpu.VMEM(gate_up_weight.shape, jnp.bfloat16),
            pltpu.VMEM(down_weight.shape, jnp.bfloat16),
            pltpu.VMEM((halves, rows, hidden), jnp.bfloat16),
            pltpu.VMEM((halves, rows, hidden), jnp.bfloat16),
            pltpu.VMEM((devices, local, count), jnp.float32),
            pltpu.VMEM((devices, local * SLOT, count), jnp.bfloat16),
            pltpu.VMEM((local, rows, LANES), jnp.float32),
            pltpu.VMEM((lines, count, half), jnp.bfloat16),
            pltpu.VMEM((lines, count, half), jnp.bfloat16),
            pltpu.VMEM((lines, count, half), jnp.bfloat16),
            pltpu.VMEM((count, half), jnp.float32),
            dma((6,)), dma((halves,)), dma((halves,)),
            dma((2,)), dma((2,)), dma((2,)), dma((2,)),
            dma((devices, 4)), dma((devices,)), dma((devices,)),
            dma((devices,)), dma((devices,)),
            dma((devices,)), dma((devices,)), dma((devices, 4)), dma((devices,)), dma((devices,)),
            dma((halves,)), dma((halves,)),
            *[dma((lines, PIECES))] * 6,
        ],
        compiler_params=pltpu.CompilerParams(
            collective_id=1, has_side_effects=True, vmem_limit_bytes=VMEM_BYTES
        ),
    )(*own, gate_up_weight, down_weight)


def body(
    tokens,
    query_key_value,
    out_weight,
    modulation,
    router_weight,
    expert_ids,
    gate_up_weight,
    down_weight,
):
    count = tokens.shape[0]
    width = tokens.shape[1]
    parts = lax.axis_size("sub")
    part = lax.axis_index("sub")
    position = lax.axis_index("dev")
    devices = lax.axis_size("dev")
    total = count * devices
    local_width = query_key_value.shape[2]
    weight_bytes = 2 * (gate_up_weight.size + down_weight.size)
    token_bytes = 12 * devices * count * width
    fits = weight_bytes + token_bytes < VMEM_BYTES and CAP <= SLOT
    paired = parts == 2 and lax.axis_size("groups") == 2 and devices % COLS == 0
    tiled = out_weight.shape[0] % (2 * LANES) == 0 and count == LANES
    if fits and paired and tiled:
        return block_call(
            tokens, query_key_value, out_weight, modulation, router_weight, expert_ids,
            gate_up_weight, down_weight,
        )
    heads_here = local_width // HEAD
    query = query_key_value[:, 0].reshape(count, heads_here, HEAD)
    pair = query_key_value[:, 1:]
    near = extended(pair, (("dev", 0),), count)
    keys = near[:, 0].reshape(3 * count, heads_here, HEAD)
    values = near[:, 1].reshape(3 * count, heads_here, HEAD)
    mixed = window_attention(query, keys, values, position, total).reshape(count, local_width)
    partial_proj = lax.dot_general(
        mixed,
        lax.all_gather(out_weight, "dev", axis=0, tiled=True),
        (((1,), (1,)), ((), ())),
        preferred_element_type=jnp.float32,
    )
    proj = lax.psum(partial_proj, "sub")
    state = tokens.astype(jnp.float32) + (1.0 + modulation[0]) * proj
    normed = normalize(state, modulation)
    gates = route(normed, router_weight, expert_ids)
    experts = router_weight.shape[1]
    topk = expert_ids.shape[1]
    flat = expert_ids.reshape(-1)
    picks = flat.shape[0]
    onehot = (flat[:, None] == jnp.arange(experts, dtype=jnp.int32)[None, :]).astype(jnp.int32)
    rank = jnp.sum((jnp.cumsum(onehot, 0) - 1) * onehot, 1)
    target = flat * CAP + rank
    hit = target[None, :] == jnp.arange(experts * CAP, dtype=jnp.int32)[:, None]
    filled = jnp.any(hit, 1)
    anchor = jnp.sum(jnp.where(hit, jnp.arange(picks, dtype=jnp.int32)[None, :], 0), 1) // topk
    slice_width = width // parts
    sent = lax.dynamic_slice_in_dim(normed, part * slice_width, slice_width, 1)
    sent_width = sent.shape[1]
    rows_out = jnp.where(filled[:, None], sent[anchor], jnp.zeros((), jnp.bfloat16))
    halves_here = gate_up_weight.shape[0]
    doubled = jnp.broadcast_to(
        rows_out.reshape(experts, 1, CAP, sent_width), (experts, 2, CAP, sent_width)
    )
    outgoing = doubled.reshape(devices, halves_here, CAP, sent_width)
    up_form = "sxcd,xgdf->sxcgf"
    down_form = "sxcf,xfd->sxcd"
    incoming = lax.all_to_all(outgoing, "dev", split_axis=0, concat_axis=0, tiled=True)
    both = jnp.einsum(
        up_form,
        lax.all_gather(incoming, "sub", axis=3, tiled=True),
        gate_up_weight,
        preferred_element_type=jnp.float32,
    )
    hidden = (jax.nn.silu(both[..., 0, :]) * both[..., 1, :]).astype(jnp.bfloat16)
    gathered = lax.all_gather(hidden, "sub", axis=hidden.ndim - 1, tiled=True)
    result = jnp.einsum(down_form, gathered, down_weight, preferred_element_type=jnp.float32)
    returned = lax.all_to_all(
        result.astype(jnp.bfloat16), "dev", split_axis=0, concat_axis=0, tiled=True
    )
    own_width = returned.shape[-1]
    arranged = returned.reshape(experts, 2, CAP, own_width)
    answers = arranged[flat, :, rank, :].reshape(count, topk, 2, own_width).astype(jnp.float32)
    combined = answers[:, :, 0] + answers[:, :, 1]
    routed = jnp.einsum("tk,tkd->td", gates, combined)
    own = lax.dynamic_slice_in_dim(state, part * slice_width, slice_width, 1)
    lift = lax.dynamic_slice_in_dim(modulation[3], part * slice_width, slice_width, 0)
    return (own + (1.0 + lift) * routed).astype(jnp.bfloat16)


def solution(mesh):
    return jax.shard_map(
        body,
        mesh=mesh,
        in_specs=(
            P(("groups", "dev"), None),
            P(("groups", "dev"), None, "sub"),
            P("dev", "sub"),
            P("groups", None),
            P(),
            P(("groups", "dev"), None),
            P("dev", None, None, "sub"),
            P("dev", None, "sub"),
        ),
        out_specs=P(("groups", "dev"), "sub"),
        check_vma=False,
    )
```
